256 devices in a mesh: order: 64 (over z, x, core), lat: 4 (over y).
Axes of the slice: x: 4, y: 4, z: 8, core: 2. Of those that a mesh axis runs over, the one named last changes fastest.
Arguments:
- position: float32 [128, 2, 64, 2160], P('order', None, None, 'lat'), may hold values from -6 to 6
- residual: float32 [128, 2, 64, 2160], P('order', None, None, 'lat'), as said below
- direction: float32 [128, 2, 64, 2160], P('order', None, None, 'lat'), as said below
- legendre: float32 [128, 2160, 2048], P('order', None, 'lat'), may hold values from -0.125 to 0.125
- order_of: int32 [128], replicated, may hold values from 0 to 2032, as said below
- class_idx: int32 [2048, 4320], P(('lat', 'order')), may hold values from 0 to 15
- land: int32 [2048, 4320], P(('lat', 'order')), may hold values 0 or 1
- class_weight: float32 [16, 2], replicated, may hold values from 0.2 to 5
- damping: float32 [2160], P('lat'), may hold values from 0.05 to 0.5
Outputs:
- new_position: float32 [128, 2, 64, 2160], P('order', None, None, 'lat')
- new_residual: float32 [128, 2, 64, 2160], P('order', None, None, 'lat')
- new_direction: float32 [128, 2, 64, 2160], P('order', None, None, 'lat')
The draws below stay inside these ranges and needn't reach their ends.
Inputs may be any that keep to these rules, and one draw needn't show every extreme that they name: `order_of`: distinct multiples of 16: each of 0, 16, ..., 16 * (128 - 1) appears exactly once. `residual`: real-valued and not zero. `direction`: real-valued and not zero.
All inputs are finite; a program needn't handle non-finite values. No bound on the sum of `land` on one device may be relied on, other than what follows from the above.
Results may differ from the reference program's by a relative error of at most 0.000058.
Values sent between devices are 32-bit elements; how exact they have to be, the bound alone decides.
A program may use at most 128 MiB of HBM per device.

```python
import math
import jax
import jax.numpy as jnp
from jax import lax

NDEG = 2160
NLON = 4320
CLASSES = 16
SAMPLES = 64
R_DEV = 8
ORDERS = 128
STRIDE = 16
NLAT = 2048


def draw_order_of(key, part):
    shuffled = jax.random.permutation(jax.random.fold_in(key, 11), ORDERS).astype(jnp.int32)
    return (shuffled * STRIDE).astype(jnp.int32)


def coefficient_field(key):
    k_base, k_rows, k_cols = jax.random.split(key, 3)
    slot_pos = jnp.arange(ORDERS, dtype=jnp.float32) / max(ORDERS - 1, 1)
    degree_pos = jnp.arange(NDEG, dtype=jnp.float32) / (NDEG - 1)
    row_scale = 3.0 ** slot_pos * 10.0 ** jax.random.uniform(k_rows, (ORDERS,), dtype=jnp.float32)
    col_scale = 3.0 ** degree_pos * 10.0 ** jax.random.uniform(k_cols, (NDEG,), dtype=jnp.float32)
    full_shape = (ORDERS, 2, SAMPLES, NDEG)
    base_draw = jax.random.normal(k_base, full_shape, dtype=jnp.float32)
    return base_draw * row_scale[:, None, None, None] * col_scale[None, None, None, :] / 30.0


def draw_residual(key, part):
    return coefficient_field(jax.random.fold_in(key, 21))


def draw_direction(key, part):
    return coefficient_field(jax.random.fold_in(key, 37))


def place_ends(array, own_key, least, high):
    longest = array.shape.index(max(array.shape))
    spots = []
    for shift in (0, 1):
        where = [jax.random.randint(jax.random.fold_in(own_key, axis), (), 0, length) for axis, length in enumerate(array.shape)]
        where[longest] = (where[longest] + shift) % array.shape[longest]
        spots.append(tuple(where))
    return array.at[spots[0]].set(least).at[spots[1]].set(high)


def block_scale(own_key, extent, pieces, least, top_value):
    factor_of, own = 1.0, jax.random.fold_in(own_key, 6)
    for dim, blocks in pieces:
        steps = jnp.exp(jax.random.uniform(jax.random.fold_in(own, dim), (blocks,), jnp.float32, least / len(pieces), top_value / len(pieces)))
        factor_of = factor_of * jnp.repeat(steps, extent[dim] // blocks).reshape([-1 if axis == dim else 1 for axis in range(len(extent))])
    return factor_of


def centred(key, extent, scale, limit, shards=(), held_as=jnp.bfloat16):
    result = jax.random.normal(key, extent, jnp.float32) * scale
    if len(shards) > 0:
        result = block_scale(key, extent, shards, -0.22, 0.18) * result
    return jnp.clip(result, min=-limit, max=limit).astype(held_as)


def setup_inputs(seed: int = 0) -> dict:
    splits = jax.random.split(jax.random.key(seed), 10)
    return {
        "position": centred(splits[0], (ORDERS, 2, SAMPLES, NDEG), 1.0, 6.0, ((0, 64), (3, 4)), jnp.float32),
        "residual": draw_residual(jax.random.fold_in(splits[9], 71), 0),
        "direction": draw_direction(jax.random.fold_in(splits[9], 71), 0),
        "legendre": centred(splits[3], (ORDERS, NDEG, NLAT), NDEG ** -0.5, 0.125, ((0, 64), (2, 4)), jnp.float32),
        "order_of": draw_order_of(jax.random.fold_in(splits[9], 71), 0),
        "class_idx": place_ends(jax.random.randint(splits[5], (NLAT, NLON), 0, CLASSES), jax.random.fold_in(splits[5], 1), 0, CLASSES - 1).astype(jnp.int32),
        "land": place_ends((jax.random.randint(splits[6], (NLAT, NLON), 0, 10) < 3).astype(jnp.int32), jax.random.fold_in(splits[6], 1), 0, 1),
        "class_weight": jnp.clip(jnp.exp(jax.random.uniform(splits[7], (CLASSES, 2), jnp.float32, math.log(0.2), math.log(5.0))), 0.2, 5.0),
        "damping": jnp.clip(jnp.exp(math.log(0.5) - 2.3025851 * jax.random.uniform(splits[8], (NDEG,), jnp.float32) ** block_scale(splits[8], (NDEG,), ((0, 4),), -0.2, 0.2)), 0.05, 0.5),
    }


def tables(order_of, longitudes):
    longitude = jnp.arange(longitudes, dtype=jnp.int32)
    phases = (order_of[:, None] * longitude[None, :]) % longitudes
    angles = phases.astype(jnp.float32) * (2.0 * math.pi / longitudes)
    return jnp.stack([jnp.cos(angles), jnp.sin(angles)])


def sample_sums(product):
    return jnp.sum(product, axis=(0, 1, 3))


def reference(position, residual, direction, legendre, order_of, class_idx, land, class_weight, damping):
    highest = lax.Precision.HIGHEST
    degrees = jnp.arange(NDEG, dtype=jnp.int32)
    in_triangle = (degrees[None, :] >= order_of[:, None]).astype(jnp.float32)[:, None, None, :]
    pos_m = position * in_triangle
    res_m = residual * in_triangle
    dir_m = direction * in_triangle
    synthesis = jnp.einsum("mskd,mdt->tmsk", dir_m, legendre, precision=highest)
    harmonic = tables(order_of, NLON)
    by_class = class_weight[class_idx]
    weight_grid = jnp.where(land == 1, by_class[:, :, 1], by_class[:, :, 0])
    count_blocks = NLAT // R_DEV

    def per_block(operands):
        rows_in, weights_in = operands
        surface = jnp.einsum("rmsk,sml->rkl", rows_in, harmonic, precision=highest)
        weighted = surface * weights_in[:, None, :]
        return jnp.einsum("rkl,sml->rmsk", weighted, harmonic, precision=highest) * (2.0 / NLON)

    spectra = lax.map(per_block, (synthesis.reshape(count_blocks, R_DEV, ORDERS, 2, SAMPLES),
                                  weight_grid.reshape(count_blocks, R_DEV, NLON)))
    spectra = spectra.reshape(NLAT, ORDERS, 2, SAMPLES)
    summed = jnp.einsum("tmsk,mdt->mskd", spectra, legendre, precision=highest)
    applied = (summed + damping[None, None, None, :] * dir_m) * in_triangle
    norm_before = sample_sums(res_m * res_m)
    curvature = sample_sums(dir_m * applied)
    step_size = (norm_before / curvature)[None, None, :, None]
    new_position = pos_m + step_size * dir_m
    new_residual = res_m - step_size * applied
    norm_after = sample_sums(new_residual * new_residual)
    ratio_new = (norm_after / norm_before)[None, None, :, None]
    new_direction = new_residual + ratio_new * dir_m
    return (new_position, new_residual, new_direction)
```

```python
import functools
import math

import jax
import jax.numpy as jnp
from jax import lax
from jax.experimental import pallas as pl
from jax.experimental.pallas import tpu as pltpu
from jax.sharding import PartitionSpec as P

F32 = jnp.float32
BF16 = jnp.bfloat16
MESH = pl.DeviceIdType.MESH

NO = 64
NL = 4
DEG = 540
SLOT = 544
HALF = SLOT // 2
WIDE = 640
STARTS = (0, 536, 1080, 1616)
BAND = 512
CH = 2
KC = 32
PERIOD = 270
NLON = 4320
ROWS_J = 272


def tall_to_wide(x):
    n = x.shape[0] // 128
    return jnp.concatenate([x[128 * i : 128 * (i + 1)].T for i in range(n)], axis=1)


def wide_to_tall(x):
    n = x.shape[1] // 128
    return jnp.concatenate([x[:, 128 * i : 128 * (i + 1)].T for i in range(n)], axis=0)


def split(x):
    hi = x.astype(BF16)
    lo = (x - hi.astype(F32)).astype(BF16)
    return hi, lo


def mm(a, b):
    return jnp.dot(a, b, preferred_element_type=F32)


def iota(shape, axis):
    return lax.broadcasted_iota(jnp.int32, shape, axis)


def fold4(x):
    y = x + pltpu.roll(x, 64, 1)
    return y + pltpu.roll(y, 32, 1)


def row_sum(x):
    acc = x[:, 0:128]
    for i in range(1, WIDE // 128):
        acc = acc + x[:, 128 * i : 128 * (i + 1)]
    return jnp.sum(acc.T, axis=0, keepdims=True)


def column(row):
    return jnp.broadcast_to(row, (128, 128)).T


def kernel(
    pos_h, res_h, dir_h, leg_h, cls_h, land_h, order_s, order_v, cw_s, damp_v,
    npos_h, nres_h, ndir_h,
    lf, lh, ll, dir_v, res_v, pos_v, cls_v, land_v, wv,
    dn, dampp, g, sy, r, t, q, pp, ra, rb, v1, v2, nres_v,
    hth, htl, hh, hl, wx, rs_acc,
    lsem, isem, osem, ag_s, ag_r, a2_s, a2_r, b2_s, b2_r, rs_s, rs_r, v1_s, v1_r, v2_s, v2_r,
):
    o = lax.axis_index("order")
    l = lax.axis_index("lat")
    right = lax.rem(l + 1, NL)
    left = lax.rem(l + NL - 1, NL)
    opp = lax.rem(l + 2, NL)
    odd = lax.rem(l, 2)

    in_dir = pltpu.make_async_copy(dir_h, dir_v, isem.at[0])
    in_dir.start()
    leg_in = []
    for b in range(NL):
        for m in range(2):
            c = pltpu.make_async_copy(
                leg_h.at[m, pl.ds(STARTS[b], SLOT), :], lf.at[m, b], lsem.at[2 * b + m]
            )
            c.start()
            leg_in.append(c)
    in_res = pltpu.make_async_copy(res_h, res_v, isem.at[1])
    in_pos = pltpu.make_async_copy(pos_h, pos_v, isem.at[2])
    in_cls = pltpu.make_async_copy(cls_h, cls_v, isem.at[3])
    in_land = pltpu.make_async_copy(land_h, land_v, isem.at[4])
    for c in (in_res, in_pos, in_cls, in_land):
        c.start()

    barrier = pltpu.get_barrier_semaphore()

    def greet(i, carry):
        peer = lax.rem(o + i, NO)
        pl.semaphore_signal(barrier, inc=1, device_id=(peer, l), device_id_type=MESH)
        return carry

    for i in range(1, NL):
        pl.semaphore_signal(
            barrier, inc=1, device_id=(o, lax.rem(l + i, NL)), device_id_type=MESH
        )
    lax.fori_loop(1, NO, greet, 0)

    row = iota((128, WIDE), 0)
    lane = iota((128, WIDE), 1)
    order_row = jnp.where(row < 64, order_s[2 * o], order_s[2 * o + 1])
    valid = (lane < DEG) & (lane + l * DEG >= order_row)

    def natural(ref, c):
        return jnp.concatenate(
            [ref[m, s, c * KC : (c + 1) * KC, :] for m in range(2) for s in range(2)],
            axis=0,
        )

    in_dir.wait()
    for c in range(CH):
        dn[c, :, 512:WIDE] = jnp.zeros((128, 128), F32)
        dn[c, :, 0:DEG] = natural(dir_v, c)
        x = jnp.where(valid, dn[c], 0.0)
        dn[c] = x
        shifted = jnp.where(odd == 1, pltpu.roll(x, 4, 1), x)
        g[c, l] = wide_to_tall(shifted)[0:SLOT]

    pl.semaphore_wait(barrier, NO - 1 + NL - 1)

    def ag(c, k, slot, lo, to):
        return pltpu.make_async_remote_copy(
            src_ref=g.at[c, slot, pl.ds(lo, HALF), :],
            dst_ref=g.at[c, slot, pl.ds(lo, HALF), :],
            send_sem=ag_s.at[c, k],
            recv_sem=ag_r.at[c, k],
            device_id=(o, to),
            device_id_type=MESH,
        )

    def ag_first(c):
        ag(c, 0, l, 0, right).start()
        ag(c, 1, l, HALF, left).start()
        ag(c, 2, l, HALF, right).start()
        ag(c, 3, l, 0, left).start()

    def ag_forward(c):
        ag(c, 0, left, 0, right).wait_recv()
        ag(c, 4, left, 0, right).start()
        ag(c, 1, right, HALF, left).wait_recv()
        ag(c, 5, right, HALF, left).start()

    ag_first(0)

    def convert(b, m):
        leg_in[2 * b + m].wait()

        def body(i, carry):
            at = pl.ds(pl.multiple_of(i * 32, 32), 32)
            hi, lo = split(lf[m, b, at, :])
            lh[m, b, at, :] = hi
            ll[m, b, at, :] = lo
            return carry

        lax.fori_loop(0, SLOT // 32, body, 0)

    for b in range(NL // 2):
        for m in range(2):
            convert(b, m)

    ag_forward(0)
    ag_first(1)

    for b in range(NL // 2, NL):
        for m in range(2):
            convert(b, m)

    col = iota((128, 256), 1)
    pick = (iota((128, 256), 0) == 2 * (col & 63) + (col >> 7)).astype(F32)
    sixteenth = jnp.broadcast_to(order_v[...].astype(F32) * (1.0 / 16.0), (8, 128))
    orders = mm(sixteenth.astype(BF16), pick.astype(BF16))[0:1, :] * 16.0
    j = iota((384, 256), 0).astype(F32)
    turns = j * orders
    phase = turns - jnp.floor(turns * (1.0 / NLON)) * float(NLON)
    part = (iota((384, 256), 1) >> 6) & 1
    phase = phase - jnp.where(part == 1, float(NLON // 4), 0.0)
    table = jnp.cos(phase * (2.0 * math.pi / NLON))
    hi, lo = split(table)
    hth[...] = hi[0:ROWS_J]
    htl[...] = lo[0:ROWS_J]
    flat = jnp.concatenate([tall_to_wide(table[:, 0:128]), tall_to_wide(table[:, 128:256])], 0)
    hi, lo = split(flat)
    hh[...] = hi[:, 0:ROWS_J]
    hl[...] = lo[:, 0:ROWS_J]

    in_cls.wait()
    in_land.wait()
    wv[:, 4224:4608] = jnp.zeros((8, 384), F32)
    for lo_lane in range(0, NLON, 640):
        n = min(640, NLON - lo_lane)
        cls = cls_v[:, lo_lane : lo_lane + n]
        on_land = land_v[:, lo_lane : lo_lane + n] == 1
        w = jnp.zeros((8, n), F32)
        for k in range(16):
            w = jnp.where(cls == k, jnp.where(on_land, cw_s[k, 1], cw_s[k, 0]), w)
        wv[:, lo_lane : lo_lane + n] = w
    folded = jnp.zeros((8, 512), F32)
    for i in range(NLON // PERIOD):
        base = PERIOD * i // 128 * 128
        off = PERIOD * i - base
        v = wv[:, base : base + 512]
        if off:
            v = pltpu.roll(v, 512 - off, 1)
        folded = folded + v
    folded = jnp.where(iota((8, 512), 1) < PERIOD, folded, 0.0) * (2.0 / NLON)
    folded = jnp.concatenate([folded[:, 0:384], jnp.zeros((120, 384), F32)], axis=0)
    spread = (iota((128, 256), 0) == (iota((128, 256), 1) >> 5)).astype(F32)
    wx[...] = jnp.dot(
        wide_to_tall(folded), spread, precision=lax.Precision.HIGHEST, preferred_element_type=F32
    )[0:ROWS_J]

    dampp[:, 512:WIDE] = jnp.zeros((1, 128), F32)
    dampp[:, 0:DEG] = damp_v[...]

    in_res.wait()
    norm_before = []
    damped = []
    for c in range(CH):
        nres_v[c, :, 512:WIDE] = jnp.zeros((128, 128), F32)
        nres_v[c, :, 0:DEG] = natural(res_v, c)
        x = jnp.where(valid, nres_v[c], 0.0)
        nres_v[c] = x
        norm_before.append(row_sum(x * x))
        y = dn[c]
        damped.append(row_sum(y * (y * dampp[...])))

    def synth(c, slot, first):
        x = jnp.concatenate([g[c, slot], jnp.zeros((WIDE - SLOT, 128), F32)], axis=0)
        wide = tall_to_wide(x)[:, 0:SLOT]
        hi, lo = split(wide)
        for m in range(2):
            a = 64 * m
            both = mm(
                jnp.concatenate([hi[a : a + 64], lo[a : a + 64]], axis=0), lh[m, slot]
            )
            out = both[0:64] + both[64:128] + mm(hi[a : a + 64], ll[m, slot])
            if first:
                rs_acc[a : a + 64, :] = out
            else:
                rs_acc[a : a + 64, :] = rs_acc[a : a + 64, :] + out

    def all_to_all(src, dst, c, ssem, rsem):
        def body(i, carry):
            peer = lax.rem(o + i, NO)
            pltpu.make_async_remote_copy(
                src_ref=src.at[c, pl.ds(pl.multiple_of(peer * 8, 8), 8), :],
                dst_ref=dst.at[c, pl.ds(pl.multiple_of(o * 8, 8), 8), :],
                send_sem=ssem.at[c],
                recv_sem=rsem.at[c],
                device_id=(peer, l),
                device_id_type=MESH,
            ).start()
            return carry

        lax.fori_loop(1, NO, body, 0)
        at = pl.ds(pl.multiple_of(o * 8, 8), 8)
        dst[c, at, :] = src[c, at, :]

    def take_all(ref, c, sem):
        part_ref = ref.at[c, pl.ds(0, 8 * (NO - 1)), :]
        pltpu.make_async_copy(part_ref, part_ref, sem.at[c]).wait()

    def synth_near(c):
        synth(c, l, True)
        ag(c, 2, left, HALF, right).wait_recv()
        synth(c, left, False)
        ag(c, 3, right, 0, left).wait_recv()
        synth(c, right, False)

    def synth_far(c):
        ag(c, 4, opp, 0, right).wait_recv()
        ag(c, 5, opp, HALF, left).wait_recv()
        synth(c, opp, False)
        sy[c] = wide_to_tall(rs_acc[...])
        all_to_all(sy, r, c, a2_s, a2_r)

    def reduce_start(i, value):
        v1[i, o] = value

        def body(k, carry):
            peer = lax.rem(o + k, NO)
            pltpu.make_async_remote_copy(
                src_ref=v1.at[i, o],
                dst_ref=v1.at[i, o],
                send_sem=v1_s.at[i],
                recv_sem=v1_r.at[i],
                device_id=(peer, l),
                device_id_type=MESH,
            ).start()
            return carry

        lax.fori_loop(1, NO, body, 0)

    def v2_copy(i, k):
        return pltpu.make_async_remote_copy(
            src_ref=v2.at[i, l],
            dst_ref=v2.at[i, l],
            send_sem=v2_s.at[i],
            recv_sem=v2_r.at[i],
            device_id=(o, lax.rem(l + k, NL)),
            device_id_type=MESH,
        )

    def reduce_middle(i):
        got = v1.at[i, pl.ds(0, NO - 1)]
        pltpu.make_async_copy(got, got, v1_r.at[i]).wait()
        v2[i, l] = jnp.sum(v1[i], axis=0)
        for k in range(1, NL):
            v2_copy(i, k).start()

    def reduce_end(i):
        got = v2.at[i, pl.ds(0, NL - 1)]
        pltpu.make_async_copy(got, got, v2_r.at[i]).wait()
        return jnp.sum(v2[i], axis=0)

    group = iota((64, 128), 1) >> 5

    def grid_stage(c):
        take_all(r, c, a2_r)
        parts = [[None] * 2 for _ in range(4)]
        for tt in range(8):
            x = r[c, pl.ds(tt, NO, stride=8), :]
            u = tt % 4
            for p in range(4):
                y = pltpu.roll(x, 32 * ((u - p) % 4), 1) if u != p else x
                old = parts[p][tt // 4]
                parts[p][tt // 4] = y if old is None else jnp.where(group == u, y, old)
        mat = jnp.concatenate([jnp.concatenate(parts[p], axis=1) for p in range(4)], axis=0)
        hi, lo = split(mat)
        surface = mm(hth[...], hi) + (mm(hth[...], lo) + mm(htl[...], hi))
        weighted = wx[...] * surface
        curve = jnp.sum(weighted * surface, axis=0, keepdims=True)
        curve = curve[:, 0:128] + curve[:, 128:256]
        hi, lo = split(weighted)
        spectra = mm(hh[...], hi) + (mm(hh[...], lo) + mm(hl[...], hi))
        for tt in range(8):
            u = tt % 4
            y = None
            for p in range(4):
                x = spectra[64 * p : 64 * p + 64, 128 * (tt // 4) : 128 * (tt // 4) + 128]
                if u != p:
                    x = pltpu.roll(x, 32 * ((p - u) % 4), 1)
                y = x if y is None else jnp.where(group == p, x, y)
            t[c, pl.ds(tt, NO, stride=8), :] = y
        all_to_all(t, q, c, b2_s, b2_r)
        reduce_start(c, jnp.concatenate([norm_before[c], curve + damped[c]], axis=0))

    low = iota((SLOT, 128), 1) < 64
    low_q = iota((BAND, 128), 1) < 64

    def analysis_operands(c):
        take_all(q, c, b2_r)
        x = q[c]
        hi, lo = split(x)
        hif = hi.astype(F32)
        lof = pltpu.roll(lo.astype(F32), 64, 1)
        zero = jnp.zeros_like(x)
        one = [jnp.where(low_q, hif, lof).astype(BF16), jnp.where(low_q, lof, hif).astype(BF16)]
        two = [jnp.where(low_q, hif, zero).astype(BF16), jnp.where(low_q, zero, hif).astype(BF16)]
        return one, two

    def analysis(c, slot, operands):
        one, two = operands
        p0 = mm(lh[0, slot], one[0])
        p1 = mm(lh[1, slot], one[1])
        tail = mm(ll[0, slot], two[0]) + mm(ll[1, slot], two[1])
        first = jnp.where(low, p0, p1)
        second = pltpu.roll(jnp.where(low, p1, p0), 64, 1)
        pp[c, slot] = first + second + tail

    def rs_one(c, k, lo, to):
        return pltpu.make_async_remote_copy(
            src_ref=pp.at[c, opp, pl.ds(lo, HALF), :],
            dst_ref=ra.at[c, k],
            send_sem=rs_s.at[c, k],
            recv_sem=rs_r.at[c, k],
            device_id=(o, to),
            device_id_type=MESH,
        )

    def rs_two(c, k, side, slot, lo, to):
        return pltpu.make_async_remote_copy(
            src_ref=pp.at[c, slot, pl.ds(lo, HALF), :],
            dst_ref=rb.at[c, side, pl.ds(lo, HALF), :],
            send_sem=rs_s.at[c, k],
            recv_sem=rs_r.at[c, k],
            device_id=(o, to),
            device_id_type=MESH,
        )

    def scatter_start(c):
        operands = analysis_operands(c)
        analysis(c, opp, operands)
        rs_one(c, 0, 0, right).start()
        rs_one(c, 1, HALF, left).start()
        analysis(c, right, operands)
        rs_two(c, 2, 0, right, HALF, right).start()
        analysis(c, left, operands)
        rs_two(c, 3, 1, left, 0, left).start()
        analysis(c, l, operands)

    def scatter_middle(c):
        rs_one(c, 0, 0, right).wait_recv()
        pp[c, right, 0:HALF, :] = pp[c, right, 0:HALF, :] + ra[c, 0]
        rs_two(c, 4, 0, right, 0, right).start()
        rs_one(c, 1, HALF, left).wait_recv()
        pp[c, left, HALF:SLOT, :] = pp[c, left, HALF:SLOT, :] + ra[c, 1]
        rs_two(c, 5, 1, left, HALF, left).start()

    def store(ref, c, value):
        for p in range(4):
            ref[p // 2, p % 2, c * KC : (c + 1) * KC, :] = value[32 * p : 32 * p + 32, 0:DEG]

    def scatter_end(c):
        sums = fold_sums(c)
        rs_two(c, 2, 0, right, HALF, right).wait_recv()
        rs_two(c, 3, 1, left, 0, left).wait_recv()
        rs_two(c, 4, 0, right, 0, right).wait_recv()
        rs_two(c, 5, 1, left, HALF, left).wait_recv()
        x = pp[c, l] + (rb[c, 0] + rb[c, 1])
        x = tall_to_wide(jnp.concatenate([x, jnp.zeros((WIDE - SLOT, 128), F32)], axis=0))
        x = jnp.where(odd == 1, pltpu.roll(x, WIDE - 4, 1), x)
        y = dn[c]
        applied = jnp.where(valid, x + dampp[...] * y, 0.0)
        step = jnp.concatenate([column(sums[0:1] / sums[1:2])] * (WIDE // 128), axis=1)
        new_res = nres_v[c] - step * applied
        nres_v[c] = new_res
        z = row_sum(new_res * new_res)
        reduce_start(CH + c, jnp.concatenate([z, z], axis=0))
        store(res_v, c, new_res)
        sy_pos = natural(pos_v, c)
        masked = jnp.where(valid[:, 0:DEG], sy_pos, 0.0)
        new_pos = masked + (step * y)[:, 0:DEG]
        store(pos_v, c, new_pos)

    def fold_sums(c):
        return fold4(reduce_end(c))

    def finish(c):
        after = fold4(reduce_end(CH + c))[0:1]
        before = fold4(jnp.sum(v2[c], axis=0))[0:1]
        ratio = jnp.concatenate([column(after / before)] * (WIDE // 128), axis=1)
        store(dir_v, c, nres_v[c] + ratio * dn[c])

    synth_near(0)
    synth_far(0)
    ag_forward(1)
    synth_near(1)
    grid_stage(0)
    synth_far(1)
    reduce_middle(0)
    scatter_start(0)
    grid_stage(1)
    scatter_middle(0)
    reduce_middle(1)
    scatter_start(1)
    in_pos.wait()
    scatter_end(0)
    scatter_middle(1)
    reduce_middle(CH)
    scatter_end(1)
    out_res = pltpu.make_async_copy(res_v, nres_h, osem.at[0])
    out_pos = pltpu.make_async_copy(pos_v, npos_h, osem.at[1])
    out_res.start()
    out_pos.start()
    finish(0)
    reduce_middle(CH + 1)
    finish(1)
    out_dir = pltpu.make_async_copy(dir_v, ndir_h, osem.at[2])
    out_dir.start()

    for c in range(CH):
        ag(c, 0, l, 0, right).wait_send()
        ag(c, 1, l, HALF, left).wait_send()
        ag(c, 2, l, HALF, right).wait_send()
        ag(c, 3, l, 0, left).wait_send()
        ag(c, 4, left, 0, right).wait_send()
        ag(c, 5, right, HALF, left).wait_send()
        rs_one(c, 0, 0, right).wait_send()
        rs_one(c, 1, HALF, left).wait_send()
        rs_two(c, 2, 0, right, HALF, right).wait_send()
        rs_two(c, 3, 1, left, 0, left).wait_send()
        rs_two(c, 4, 0, right, 0, right).wait_send()
        rs_two(c, 5, 1, left, HALF, left).wait_send()
        take_all(sy, c, a2_s)
        take_all(t, c, b2_s)
    for i in range(2 * CH):
        sent = v1.at[i, pl.ds(0, NO - 1)]
        pltpu.make_async_copy(sent, sent, v1_s.at[i]).wait()
        sent = v2.at[i, pl.ds(0, NL - 1)]
        pltpu.make_async_copy(sent, sent, v2_s.at[i]).wait()
    out_res.wait()
    out_pos.wait()
    out_dir.wait()


def shards(
    position, residual, direction, legendre, order_of, class_idx, land, class_weight, damping
):
    any_spec = pl.BlockSpec(memory_space=pl.ANY)
    smem = pl.BlockSpec(memory_space=pltpu.SMEM)
    vmem = pl.BlockSpec(memory_space=pltpu.VMEM)
    dma = pltpu.SemaphoreType.DMA
    block = (2, 2, 64, DEG)
    return pl.pallas_call(
        kernel,
        out_shape=[jax.ShapeDtypeStruct(block, F32)] * 3,
        in_specs=[any_spec] * 6 + [smem, vmem, smem, vmem],
        out_specs=[any_spec] * 3,
        scratch_shapes=[
            pltpu.VMEM((2, NL, SLOT, BAND), F32),
            pltpu.VMEM((2, NL, SLOT, BAND), BF16),
            pltpu.VMEM((2, NL, SLOT, BAND), BF16),
            pltpu.VMEM(block, F32),
            pltpu.VMEM(block, F32),
            pltpu.VMEM(block, F32),
            pltpu.VMEM((8, NLON), jnp.int32),
            pltpu.VMEM((8, NLON), jnp.int32),
            pltpu.VMEM((8, 4608), F32),
            pltpu.VMEM((CH, 128, WIDE), F32),
            pltpu.VMEM((1, WIDE), F32),
            pltpu.VMEM((CH, NL, SLOT, 128), F32),
            pltpu.VMEM((CH, BAND, 128), F32),
            pltpu.VMEM((CH, BAND, 128), F32),
            pltpu.VMEM((CH, BAND, 128), F32),
            pltpu.VMEM((CH, BAND, 128), F32),
            pltpu.VMEM((CH, NL, SLOT, 128), F32),
            pltpu.VMEM((CH, 2, HALF, 128), F32),
            pltpu.VMEM((CH, 2, SLOT, 128), F32),
            pltpu.VMEM((2 * CH, NO, 2, 128), F32),
            pltpu.VMEM((2 * CH, NL, 2, 128), F32),
            pltpu.VMEM((CH, 128, WIDE), F32),
            pltpu.VMEM((ROWS_J, 256), BF16),
            pltpu.VMEM((ROWS_J, 256), BF16),
            pltpu.VMEM((256, ROWS_J), BF16),
            pltpu.VMEM((256, ROWS_J), BF16),
            pltpu.VMEM((ROWS_J, 256), F32),
            pltpu.VMEM((128, BAND), F32),
            dma((8,)),
            dma((5,)),
            dma((3,)),
            dma((CH, 6)),
            dma((CH, 6)),
            dma((CH,)),
            dma((CH,)),
            dma((CH,)),
            dma((CH,)),
            dma((CH, 6)),
            dma((CH, 6)),
            dma((2 * CH,)),
            dma((2 * CH,)),
            dma((2 * CH,)),
            dma((2 * CH,)),
        ],
        compiler_params=pltpu.CompilerParams(
            collective_id=0, has_side_effects=True, vmem_limit_bytes=60 * 1024 * 1024
        ),
        name="cg_iteration",
    )(
        position, residual, direction, legendre, class_idx, land,
        order_of, order_of.reshape(1, -1), class_weight, damping.reshape(1, -1),
    )


def solution(mesh):
    return jax.shard_map(
        shards,
        mesh=mesh,
        in_specs=(
            P("order", None, None, "lat"),
            P("order", None, None, "lat"),
            P("order", None, None, "lat"),
            P("order", None, "lat"),
            P(),
            P(("lat", "order"), None),
            P(("lat", "order"), None),
            P(),
            P("lat"),
        ),
        out_specs=(
            P("order", None, None, "lat"),
            P("order", None, None, "lat"),
            P("order", None, None, "lat"),
        ),
        check_vma=False,
    )
```

```python
import functools
import math

import jax
import jax.numpy as jnp
from jax import lax
from jax.experimental import pallas as pl
from jax.experimental.pallas import tpu as pltpu
from jax.sharding import PartitionSpec as P

F32 = jnp.float32
BF16 = jnp.bfloat16
MESH = pl.DeviceIdType.MESH

NO = 64
NL = 4
DEG = 540
SLOT = 544
HALF = SLOT // 2
WIDE = 640
STARTS = (0, 536, 1080, 1616)
BAND = 512
CH = 2
KC = 32
PERIOD = 270
NLON = 4320
ROWS_J = 272


def tall_to_wide(x):
    n = x.shape[0] // 128
    return jnp.concatenate([x[128 * i : 128 * (i + 1)].T for i in range(n)], axis=1)


def wide_to_tall(x):
    n = x.shape[1] // 128
    return jnp.concatenate([x[:, 128 * i : 128 * (i + 1)].T for i in range(n)], axis=0)


def split(x):
    hi = x.astype(BF16)
    lo = (x - hi.astype(F32)).astype(BF16)
    return hi, lo


def mm(a, b):
    return jnp.dot(a, b, preferred_element_type=F32)


def iota(shape, axis):
    return lax.broadcasted_iota(jnp.int32, shape, axis)


def fold4(x):
    y = x + pltpu.roll(x, 64, 1)
    return y + pltpu.roll(y, 32, 1)


def column(row):
    return jnp.broadcast_to(row, (128, 128)).T


def kernel(
    res_h, dir_h, leg_h, cls_h, land_h, order_h, order_w, cw_h, damp_h,
    app_h, cols_v, order_s, order_v, cw_s, damp_v,
    lf, lh, ll, dir_v, res_v, app_v, cls_v, land_v, wv,
    dn, dampp, g, sy, r, t, q, pp, ra, rb, v1, v2,
    rt, dampt, validt, hth, htl, hh, hl, wx, rs_acc,
    lsem, isem, osem, ag_s, ag_r, a2_s, a2_r, b2_s, b2_r, rs_s, rs_r, v1_s, v1_r, v2_s, v2_r,
):
    o = lax.axis_index("order")
    l = lax.axis_index("lat")
    right = lax.rem(l + 1, NL)
    left = lax.rem(l + NL - 1, NL)
    opp = lax.rem(l + 2, NL)
    odd = lax.rem(l, 2)

    in_dir = pltpu.make_async_copy(dir_h, dir_v, isem.at[0])
    in_dir.start()
    in_order = pltpu.make_async_copy(order_h, order_s, isem.at[2])
    in_order.start()
    barrier = pltpu.get_barrier_semaphore()

    def order_peer(i):
        k = i >> 3
        dz = 4 + ((k + 1) >> 1) * (1 - 2 * (k & 1))
        j = (i & 7) + ((k + 1) >> 3)
        return ((o + dz * 8) & 56) + ((o + j) & 7)

    def greet(i, carry):
        pl.semaphore_signal(
            barrier, inc=1, device_id=(order_peer(i), l), device_id_type=MESH
        )
        return carry

    for i in range(1, NL):
        pl.semaphore_signal(
            barrier, inc=1, device_id=(o, lax.rem(l + i, NL)), device_id_type=MESH
        )
    lax.fori_loop(0, NO - 1, greet, 0)

    leg_in = []
    for b in range(NL):
        for m in range(2):
            c = pltpu.make_async_copy(
                leg_h.at[m, pl.ds(STARTS[b], SLOT), :], lf.at[m, b], lsem.at[2 * b + m]
            )
            c.start()
            leg_in.append(c)
    in_res = pltpu.make_async_copy(res_h, res_v, isem.at[1])
    in_cls = pltpu.make_async_copy(cls_h, cls_v, isem.at[3])
    in_land = pltpu.make_async_copy(land_h, land_v, isem.at[4])
    in_wide = pltpu.make_async_copy(order_w, order_v, isem.at[5])
    in_cw = pltpu.make_async_copy(cw_h, cw_s, isem.at[6])
    in_damp = pltpu.make_async_copy(damp_h, damp_v, isem.at[7])
    for c in (in_wide, in_cw, in_damp, in_cls, in_land, in_res):
        c.start()
    in_order.wait()

    row = iota((128, WIDE), 0)
    lane = iota((128, WIDE), 1)
    order_row = jnp.where(row < 64, order_s[2 * o], order_s[2 * o + 1])
    valid = (lane < DEG) & (lane + l * DEG >= order_row)

    def natural(ref, c):
        return jnp.concatenate(
            [ref[m, s, c * KC : (c + 1) * KC, :] for m in range(2) for s in range(2)],
            axis=0,
        )

    def rows_of(x):
        return wide_to_tall(jnp.where(odd == 1, pltpu.roll(x, 4, 1), x))[0:SLOT]

    in_dir.wait()
    for c in range(CH):
        dn[c, :, 512:WIDE] = jnp.zeros((128, 128), F32)
        dn[c, :, 0:DEG] = natural(dir_v, c)
        g[c, l] = rows_of(jnp.where(valid, dn[c], 0.0))

    pl.semaphore_wait(barrier, NO - 1 + NL - 1)

    def ag(c, k, slot, lo, to):
        return pltpu.make_async_remote_copy(
            src_ref=g.at[c, slot, pl.ds(lo, HALF), :],
            dst_ref=g.at[c, slot, pl.ds(lo, HALF), :],
            send_sem=ag_s.at[c, k],
            recv_sem=ag_r.at[c, k],
            device_id=(o, to),
            device_id_type=MESH,
        )

    def ag_first(c):
        ag(c, 0, l, 0, right).start()
        ag(c, 1, l, HALF, left).start()
        ag(c, 2, l, HALF, right).start()
        ag(c, 3, l, 0, left).start()

    def ag_forward(c):
        ag(c, 0, left, 0, right).wait_recv()
        ag(c, 4, left, 0, right).start()
        ag(c, 1, right, HALF, left).wait_recv()
        ag(c, 5, right, HALF, left).start()

    ag_first(0)

    def convert(b, m):
        leg_in[2 * b + m].wait()

        def body(i, carry):
            at = pl.ds(pl.multiple_of(i * 32, 32), 32)
            hi, lo = split(lf[m, b, at, :])
            lh[m, b, at, :] = hi
            ll[m, b, at, :] = lo
            return carry

        lax.fori_loop(0, SLOT // 32, body, 0)

    for b in range(NL // 2):
        for m in range(2):
            convert(b, m)

    ag_forward(0)
    ag_first(1)

    for b in range(NL // 2, NL):
        for m in range(2):
            convert(b, m)

    in_wide.wait()
    in_cw.wait()
    in_damp.wait()
    col = iota((128, 256), 1)
    pick = (iota((128, 256), 0) == 2 * (col & 63) + (col >> 7)).astype(F32)
    sixteenth = jnp.broadcast_to(order_v[...].astype(F32) * (1.0 / 16.0), (8, 128))
    orders = mm(sixteenth.astype(BF16), pick.astype(BF16))[0:1, :] * 16.0
    j = iota((384, 256), 0).astype(F32)
    turns = j * orders
    phase = turns - jnp.floor(turns * (1.0 / NLON)) * float(NLON)
    part = (iota((384, 256), 1) >> 6) & 1
    phase = phase - jnp.where(part == 1, float(NLON // 4), 0.0)
    table = jnp.cos(phase * (2.0 * math.pi / NLON))
    hi, lo = split(table)
    hth[...] = hi[0:ROWS_J]
    htl[...] = lo[0:ROWS_J]
    flat = jnp.concatenate([tall_to_wide(table[:, 0:128]), tall_to_wide(table[:, 128:256])], 0)
    hi, lo = split(flat)
    hh[...] = hi[:, 0:ROWS_J]
    hl[...] = lo[:, 0:ROWS_J]

    in_cls.wait()
    in_land.wait()
    wv[:, 4224:4608] = jnp.zeros((8, 384), F32)
    for lo_lane in range(0, NLON, 640):
        n = min(640, NLON - lo_lane)
        cls = cls_v[:, lo_lane : lo_lane + n]
        on_land = land_v[:, lo_lane : lo_lane + n] == 1
        w = jnp.zeros((8, n), F32)
        for k in range(16):
            w = jnp.where(cls == k, jnp.where(on_land, cw_s[1, k], cw_s[0, k]), w)
        wv[:, lo_lane : lo_lane + n] = w
    folded = jnp.zeros((8, 512), F32)
    for i in range(NLON // PERIOD):
        base = PERIOD * i // 128 * 128
        off = PERIOD * i - base
        v = wv[:, base : base + 512]
        if off:
            v = pltpu.roll(v, 512 - off, 1)
        folded = folded + v
    folded = jnp.where(iota((8, 512), 1) < PERIOD, folded, 0.0) * (2.0 / NLON)
    folded = jnp.concatenate([folded[:, 0:384], jnp.zeros((120, 384), F32)], axis=0)
    spread = (iota((128, 256), 0) == (iota((128, 256), 1) >> 5)).astype(F32)
    wx[...] = jnp.dot(
        wide_to_tall(folded), spread, precision=lax.Precision.HIGHEST, preferred_element_type=F32
    )[0:ROWS_J]

    dampp[:, 512:WIDE] = jnp.zeros((1, 128), F32)
    dampp[:, 0:DEG] = damp_v[...].reshape(1, DEG)
    dampt[...] = rows_of(jnp.broadcast_to(dampp[...], (128, WIDE)))
    validt[...] = rows_of(valid.astype(F32))

    in_res.wait()
    norm_before = []
    damped = []
    for c in range(CH):
        dn[c, :, 0:DEG] = natural(res_v, c)
        x = rows_of(jnp.where(valid, dn[c], 0.0))
        rt[c] = x
        norm_before.append(jnp.sum(x * x, axis=0, keepdims=True))
        y = g[c, l]
        damped.append(jnp.sum(y * (y * dampt[...]), axis=0, keepdims=True))

    def synth(c, slot, first):
        x = jnp.concatenate([g[c, slot], jnp.zeros((WIDE - SLOT, 128), F32)], axis=0)
        wide = tall_to_wide(x)[:, 0:SLOT]
        hi, lo = split(wide)
        for m in range(2):
            a = 64 * m
            both = mm(
                jnp.concatenate([hi[a : a + 64], lo[a : a + 64]], axis=0), lh[m, slot]
            )
            out = both[0:64] + both[64:128] + mm(hi[a : a + 64], ll[m, slot])
            if first:
                rs_acc[a : a + 64, :] = out
            else:
                rs_acc[a : a + 64, :] = rs_acc[a : a + 64, :] + out

    def all_to_all(src, dst, c, ssem, rsem):
        def body(i, carry):
            peer = order_peer(i)
            pltpu.make_async_remote_copy(
                src_ref=src.at[c, pl.ds(pl.multiple_of(peer * 8, 8), 8), :],
                dst_ref=dst.at[c, pl.ds(pl.multiple_of(o * 8, 8), 8), :],
                send_sem=ssem.at[c],
                recv_sem=rsem.at[c],
                device_id=(peer, l),
                device_id_type=MESH,
            ).start()
            return carry

        lax.fori_loop(0, NO - 1, body, 0)
        at = pl.ds(pl.multiple_of(o * 8, 8), 8)
        dst[c, at, :] = src[c, at, :]

    def take_all(ref, c, sem):
        part_ref = ref.at[c, pl.ds(0, 8 * (NO - 1)), :]
        pltpu.make_async_copy(part_ref, part_ref, sem.at[c]).wait()

    def synth_near(c):
        synth(c, l, True)
        ag(c, 2, left, HALF, right).wait_recv()
        synth(c, left, False)
        ag(c, 3, right, 0, left).wait_recv()
        synth(c, right, False)

    def synth_far(c):
        ag(c, 4, opp, 0, right).wait_recv()
        ag(c, 5, opp, HALF, left).wait_recv()
        synth(c, opp, False)
        sy[c] = wide_to_tall(rs_acc[...])
        all_to_all(sy, r, c, a2_s, a2_r)

    def reduce_start(i, value):
        v1[i, o] = value

        def body(k, carry):
            peer = order_peer(k)
            pltpu.make_async_remote_copy(
                src_ref=v1.at[i, o],
                dst_ref=v1.at[i, o],
                send_sem=v1_s.at[i],
                recv_sem=v1_r.at[i],
                device_id=(peer, l),
                device_id_type=MESH,
            ).start()
            return carry

        lax.fori_loop(0, NO - 1, body, 0)

    def v2_copy(i, k):
        return pltpu.make_async_remote_copy(
            src_ref=v2.at[i, l],
            dst_ref=v2.at[i, l],
            send_sem=v2_s.at[i],
            recv_sem=v2_r.at[i],
            device_id=(o, lax.rem(l + k, NL)),
            device_id_type=MESH,
        )

    def reduce_middle(i):
        got = v1.at[i, pl.ds(0, NO - 1)]
        pltpu.make_async_copy(got, got, v1_r.at[i]).wait()
        v2[i, l] = jnp.sum(v1[i], axis=0)
        for k in range(1, NL):
            v2_copy(i, k).start()

    def reduce_end(i):
        got = v2.at[i, pl.ds(0, NL - 1)]
        pltpu.make_async_copy(got, got, v2_r.at[i]).wait()
        return jnp.sum(v2[i], axis=0)

    group = iota((64, 128), 1) >> 5

    def grid_stage(c):
        take_all(r, c, a2_r)
        parts = [[None] * 2 for _ in range(4)]
        for tt in range(8):
            x = r[c, pl.ds(tt, NO, stride=8), :]
            u = tt % 4
            for p in range(4):
                y = pltpu.roll(x, 32 * ((u - p) % 4), 1) if u != p else x
                old = parts[p][tt // 4]
                parts[p][tt // 4] = y if old is None else jnp.where(group == u, y, old)
        mat = jnp.concatenate([jnp.concatenate(parts[p], axis=1) for p in range(4)], axis=0)
        hi, lo = split(mat)
        surface = mm(hth[...], hi) + (mm(hth[...], lo) + mm(htl[...], hi))
        weighted = wx[...] * surface
        curve = jnp.sum(weighted * surface, axis=0, keepdims=True)
        curve = curve[:, 0:128] + curve[:, 128:256]
        hi, lo = split(weighted)
        spectra = mm(hh[...], hi) + (mm(hh[...], lo) + mm(hl[...], hi))
        for tt in range(8):
            u = tt % 4
            y = None
            for p in range(4):
                x = spectra[64 * p : 64 * p + 64, 128 * (tt // 4) : 128 * (tt // 4) + 128]
                if u != p:
                    x = pltpu.roll(x, 32 * ((p - u) % 4), 1)
                y = x if y is None else jnp.where(group == p, x, y)
            t[c, pl.ds(tt, NO, stride=8), :] = y
        all_to_all(t, q, c, b2_s, b2_r)
        reduce_start(c, jnp.concatenate([norm_before[c], curve + damped[c]], axis=0))

    low = iota((SLOT, 128), 1) < 64
    low_q = iota((BAND, 128), 1) < 64

    def analysis_operands(c):
        take_all(q, c, b2_r)
        x = q[c]
        hi, lo = split(x)
        hif = hi.astype(F32)
        lof = pltpu.roll(lo.astype(F32), 64, 1)
        zero = jnp.zeros_like(x)
        one = [jnp.where(low_q, hif, lof).astype(BF16), jnp.where(low_q, lof, hif).astype(BF16)]
        two = [jnp.where(low_q, hif, zero).astype(BF16), jnp.where(low_q, zero, hif).astype(BF16)]
        return one, two

    def analysis(c, slot, operands):
        one, two = operands
        p0 = mm(lh[0, slot], one[0])
        p1 = mm(lh[1, slot], one[1])
        tail = mm(ll[0, slot], two[0]) + mm(ll[1, slot], two[1])
        first = jnp.where(low, p0, p1)
        second = pltpu.roll(jnp.where(low, p1, p0), 64, 1)
        pp[c, slot] = first + second + tail

    def rs_one(c, k, lo, to):
        return pltpu.make_async_remote_copy(
            src_ref=pp.at[c, opp, pl.ds(lo, HALF), :],
            dst_ref=ra.at[c, k],
            send_sem=rs_s.at[c, k],
            recv_sem=rs_r.at[c, k],
            device_id=(o, to),
            device_id_type=MESH,
        )

    def rs_two(c, k, side, slot, lo, to):
        return pltpu.make_async_remote_copy(
            src_ref=pp.at[c, slot, pl.ds(lo, HALF), :],
            dst_ref=rb.at[c, side, pl.ds(lo, HALF), :],
            send_sem=rs_s.at[c, k],
            recv_sem=rs_r.at[c, k],
            device_id=(o, to),
            device_id_type=MESH,
        )

    def scatter_start(c):
        operands = analysis_operands(c)
        analysis(c, opp, operands)
        rs_one(c, 0, 0, right).start()
        rs_one(c, 1, HALF, left).start()
        analysis(c, right, operands)
        rs_two(c, 2, 0, right, HALF, right).start()
        analysis(c, left, operands)
        rs_two(c, 3, 1, left, 0, left).start()
        analysis(c, l, operands)

    def scatter_middle(c):
        rs_one(c, 0, 0, right).wait_recv()
        pp[c, right, 0:HALF, :] = pp[c, right, 0:HALF, :] + ra[c, 0]
        rs_two(c, 4, 0, right, 0, right).start()
        rs_one(c, 1, HALF, left).wait_recv()
        pp[c, left, HALF:SLOT, :] = pp[c, left, HALF:SLOT, :] + ra[c, 1]
        rs_two(c, 5, 1, left, HALF, left).start()

    def store(ref, c, value):
        for p in range(4):
            ref[p // 2, p % 2, c * KC : (c + 1) * KC, :] = value[32 * p : 32 * p + 32, 0:DEG]

    def scatter_end(c):
        sums = fold_sums(c)
        rs_two(c, 2, 0, right, HALF, right).wait_recv()
        rs_two(c, 3, 1, left, 0, left).wait_recv()
        rs_two(c, 4, 0, right, 0, right).wait_recv()
        rs_two(c, 5, 1, left, HALF, left).wait_recv()
        x = pp[c, l] + (rb[c, 0] + rb[c, 1])
        step = sums[0:1] / sums[1:2]
        applied = jnp.where(validt[...] > 0.5, x + dampt[...] * g[c, l], 0.0)
        new_res = rt[c] - step * applied
        z = jnp.sum(new_res * new_res, axis=0, keepdims=True)
        reduce_start(CH + c, jnp.concatenate([z, z], axis=0))
        x = jnp.concatenate([applied, jnp.zeros((WIDE - SLOT, 128), F32)], axis=0)
        x = tall_to_wide(x)
        x = jnp.where(odd == 1, pltpu.roll(x, WIDE - 4, 1), x)
        store(app_v, c, x)
        cols_v[0, c * KC : (c + 1) * KC, :] = column(step)[0:KC]

    def fold_sums(c):
        return fold4(reduce_end(c))

    def finish(c):
        after = fold4(reduce_end(CH + c))[0:1]
        before = fold4(jnp.sum(v2[c], axis=0))[0:1]
        cols_v[1, c * KC : (c + 1) * KC, :] = column(after / before)[0:KC]

    synth_near(0)
    synth_far(0)
    ag_forward(1)
    synth_near(1)
    synth_far(1)
    grid_stage(0)
    grid_stage(1)
    scatter_start(0)
    reduce_middle(0)
    scatter_middle(0)
    scatter_start(1)
    reduce_middle(1)
    scatter_end(0)
    scatter_middle(1)
    reduce_middle(CH)
    scatter_end(1)
    out_app = pltpu.make_async_copy(app_v, app_h, osem.at[0])
    out_app.start()
    finish(0)
    reduce_middle(CH + 1)
    finish(1)

    for c in range(CH):
        ag(c, 0, l, 0, right).wait_send()
        ag(c, 1, l, HALF, left).wait_send()
        ag(c, 2, l, HALF, right).wait_send()
        ag(c, 3, l, 0, left).wait_send()
        ag(c, 4, left, 0, right).wait_send()
        ag(c, 5, right, HALF, left).wait_send()
        rs_one(c, 0, 0, right).wait_send()
        rs_one(c, 1, HALF, left).wait_send()
        rs_two(c, 2, 0, right, HALF, right).wait_send()
        rs_two(c, 3, 1, left, 0, left).wait_send()
        rs_two(c, 4, 0, right, 0, right).wait_send()
        rs_two(c, 5, 1, left, HALF, left).wait_send()
        take_all(sy, c, a2_s)
        take_all(t, c, b2_s)
    for i in range(2 * CH):
        sent = v1.at[i, pl.ds(0, NO - 1)]
        pltpu.make_async_copy(sent, sent, v1_s.at[i]).wait()
        sent = v2.at[i, pl.ds(0, NL - 1)]
        pltpu.make_async_copy(sent, sent, v2_s.at[i]).wait()
    out_app.wait()


def combine(pos_v, res_v, dir_v, app_v, order_s, cols_v, npos_h, nres_h, ndir_h, y, osem):
    o = lax.axis_index("order")
    l = lax.axis_index("lat")
    degree = iota((64, DEG), 1) + l * DEG
    step = jnp.concatenate([cols_v[0]] * 5, axis=1)[:, 0:DEG]
    ratio = jnp.concatenate([cols_v[1]] * 5, axis=1)[:, 0:DEG]
    outs = []
    for m in range(2):
        valid = degree >= order_s[2 * o + m]
        for s in range(2):
            pos, res, way = (jnp.where(valid, x[m, s], 0.0) for x in (pos_v, res_v, dir_v))
            new_res = res - step * app_v[m, s]
            y[0, m, s] = pos + step * way
            y[1, m, s] = new_res
            y[2, m, s] = new_res + ratio * way
            for k, ref in enumerate((npos_h, nres_h, ndir_h)):
                c = pltpu.make_async_copy(y.at[k, m, s], ref.at[m, s], osem.at[k, m, s])
                c.start()
                outs.append(c)
    for c in outs:
        c.wait()


def shards(
    position, residual, direction, legendre, order_of, class_idx, land, class_weight, damping
):
    any_spec = pl.BlockSpec(memory_space=pl.ANY)
    hbm = pl.BlockSpec(memory_space=pltpu.HBM)
    smem = pl.BlockSpec(memory_space=pltpu.SMEM)
    vmem = pl.BlockSpec(memory_space=pltpu.VMEM)
    dma = pltpu.SemaphoreType.DMA
    block = (2, 2, 64, DEG)
    applied, columns = pl.pallas_call(
        kernel,
        out_shape=[jax.ShapeDtypeStruct(block, F32), jax.ShapeDtypeStruct((2, 64, 128), F32)],
        in_specs=[hbm] * 9,
        out_specs=[any_spec, vmem],
        scratch_shapes=[
            pltpu.SMEM((128,), jnp.int32),
            pltpu.VMEM((1, 128), jnp.int32),
            pltpu.SMEM((2, 16), F32),
            pltpu.VMEM((DEG,), F32),
            pltpu.VMEM((2, NL, SLOT, BAND), F32),
            pltpu.VMEM((2, NL, SLOT, BAND), BF16),
            pltpu.VMEM((2, NL, SLOT, BAND), BF16),
            pltpu.VMEM(block, F32),
            pltpu.VMEM(block, F32),
            pltpu.VMEM(block, F32),
            pltpu.VMEM((8, NLON), jnp.int32),
            pltpu.VMEM((8, NLON), jnp.int32),
            pltpu.VMEM((8, 4608), F32),
            pltpu.VMEM((CH, 128, WIDE), F32),
            pltpu.VMEM((1, WIDE), F32),
            pltpu.VMEM((CH, NL, SLOT, 128), F32),
            pltpu.VMEM((CH, BAND, 128), F32),
            pltpu.VMEM((CH, BAND, 128), F32),
            pltpu.VMEM((CH, BAND, 128), F32),
            pltpu.VMEM((CH, BAND, 128), F32),
            pltpu.VMEM((CH, NL, SLOT, 128), F32),
            pltpu.VMEM((CH, 2, HALF, 128), F32),
            pltpu.VMEM((CH, 2, SLOT, 128), F32),
            pltpu.VMEM((2 * CH, NO, 2, 128), F32),
            pltpu.VMEM((2 * CH, NL, 2, 128), F32),
            pltpu.VMEM((CH, SLOT, 128), F32),
            pltpu.VMEM((SLOT, 128), F32),
            pltpu.VMEM((SLOT, 128), F32),
            pltpu.VMEM((ROWS_J, 256), BF16),
            pltpu.VMEM((ROWS_J, 256), BF16),
            pltpu.VMEM((256, ROWS_J), BF16),
            pltpu.VMEM((256, ROWS_J), BF16),
            pltpu.VMEM((ROWS_J, 256), F32),
            pltpu.VMEM((128, BAND), F32),
            dma((8,)),
            dma((8,)),
            dma((3,)),
            dma((CH, 6)),
            dma((CH, 6)),
            dma((CH,)),
            dma((CH,)),
            dma((CH,)),
            dma((CH,)),
            dma((CH, 6)),
            dma((CH, 6)),
            dma((2 * CH,)),
            dma((2 * CH,)),
            dma((2 * CH,)),
            dma((2 * CH,)),
        ],
        compiler_params=pltpu.CompilerParams(
            collective_id=0, has_side_effects=True, vmem_limit_bytes=36 * 1024 * 1024
        ),
        name="cg_iteration",
    )(
        *(
            pltpu.with_memory_space_constraint(a, pltpu.HBM)
            for a in (
                residual, direction, legendre, class_idx, land,
                order_of, order_of.reshape(1, -1), class_weight.T, damping,
            )
        )
    )
    return pl.pallas_call(
        combine,
        out_shape=[jax.ShapeDtypeStruct(block, F32)] * 3,
        in_specs=[vmem] * 4 + [smem, vmem],
        out_specs=[any_spec] * 3,
        scratch_shapes=[
            pltpu.VMEM((3,) + block, F32),
            dma((3, 2, 2)),
        ],
        compiler_params=pltpu.CompilerParams(vmem_limit_bytes=16 * 1024 * 1024),
        name="combine",
    )(position, residual, direction, applied, order_of, columns)


def solution(mesh):
    return jax.shard_map(
        shards,
        mesh=mesh,
        in_specs=(
            P("order", None, None, "lat"),
            P("order", None, None, "lat"),
            P("order", None, None, "lat"),
            P("order", None, "lat"),
            P(),
            P(("lat", "order"), None),
            P(("lat", "order"), None),
            P(),
            P("lat"),
        ),
        out_specs=(
            P("order", None, None, "lat"),
            P("order", None, None, "lat"),
            P("order", None, None, "lat"),
        ),
        check_vma=False,
    )
```

```python
import functools
import math

import jax
import jax.numpy as jnp
from jax import lax
from jax.experimental import pallas as pl
from jax.experimental.pallas import tpu as pltpu
from jax.sharding import PartitionSpec as P

F32 = jnp.float32
BF16 = jnp.bfloat16
MESH = pl.DeviceIdType.MESH

NO = 64
NL = 4
DEG = 540
SLOT = 544
HALF = SLOT // 2
WIDE = 640
STARTS = (0, 536, 1080, 1616)
BAND = 512
CH = 2
NS = 4
KS = 16
PACK = SLOT // 2
QH = PACK // 2
PERIOD = 270
NLON = 4320
ROWS_J = 272


def tall_to_wide(x):
    n = x.shape[0] // 128
    return jnp.concatenate([x[128 * i : 128 * (i + 1)].T for i in range(n)], axis=1)


def wide_to_tall(x):
    n = x.shape[1] // 128
    return jnp.concatenate([x[:, 128 * i : 128 * (i + 1)].T for i in range(n)], axis=0)


def split(x):
    hi = x.astype(BF16)
    lo = (x - hi.astype(F32)).astype(BF16)
    return hi, lo


def mm(a, b):
    return jnp.dot(a, b, preferred_element_type=F32)


def iota(shape, axis):
    return lax.broadcasted_iota(jnp.int32, shape, axis)


def fold8(x):
    y = x + pltpu.roll(x, 64, 1)
    y = y + pltpu.roll(y, 32, 1)
    return y + pltpu.roll(y, 16, 1)


def pack(x, h):
    low = iota((PACK, 128), 1) < 64
    top, bottom = x[0:PACK], x[PACK:SLOT]
    if h == 0:
        return jnp.where(low, top, pltpu.roll(bottom, 64, 1))
    return jnp.where(low, pltpu.roll(top, 64, 1), bottom)


def column(row):
    return jnp.broadcast_to(row, (128, 128)).T


def kernel(
    res_h, dir_h, leg_h, cls_h, land_h, order_h, order_w, cw_h, damp_h,
    app_h, cols_v, order_s, order_v, cw_s, damp_v,
    lf, lh, ll, dir_v, res_v, app_v, cls_v, land_v, wv,
    dn, dampp, g, gp, xs, sy, r, t, q, pp, ra, rb, v1, v2,
    rt, dampt, validt, hth, htl, hh, hl, wx, rs_acc,
    lsem, isem, osem, ag_s, ag_r, a2_s, a2_r, b2_s, b2_r, rs_s, rs_r, v1_s, v1_r, v2_s, v2_r,
):
    o = lax.axis_index("order")
    l = lax.axis_index("lat")
    right = lax.rem(l + 1, NL)
    left = lax.rem(l + NL - 1, NL)
    opp = lax.rem(l + 2, NL)
    odd = lax.rem(l, 2)

    in_dir = pltpu.make_async_copy(dir_h, dir_v, isem.at[0])
    in_dir.start()
    in_order = pltpu.make_async_copy(order_h, order_s, isem.at[2])
    in_order.start()
    barrier = pltpu.get_barrier_semaphore()

    def order_peer(i):
        k = i >> 3
        dz = 4 + ((k + 1) >> 1) * (1 - 2 * (k & 1))
        j = (i & 7) + ((k + 1) >> 3)
        return ((o + dz * 8) & 56) + ((o + j) & 7)

    def greet(i, carry):
        pl.semaphore_signal(
            barrier, inc=1, device_id=(order_peer(i), l), device_id_type=MESH
        )
        return carry

    for i in range(1, NL):
        pl.semaphore_signal(
            barrier, inc=1, device_id=(o, lax.rem(l + i, NL)), device_id_type=MESH
        )
    lax.fori_loop(0, NO - 1, greet, 0, unroll=9)

    leg_in = []
    for b in range(NL):
        for m in range(2):
            c = pltpu.make_async_copy(
                leg_h.at[m, pl.ds(STARTS[b], SLOT), :], lf.at[m, b], lsem.at[2 * b + m]
            )
            c.start()
            leg_in.append(c)
    in_res = pltpu.make_async_copy(res_h, res_v, isem.at[1])
    in_cls = pltpu.make_async_copy(cls_h, cls_v, isem.at[3])
    in_land = pltpu.make_async_copy(land_h, land_v, isem.at[4])
    in_wide = pltpu.make_async_copy(order_w, order_v, isem.at[5])
    in_cw = pltpu.make_async_copy(cw_h, cw_s, isem.at[6])
    in_damp = pltpu.make_async_copy(damp_h, damp_v, isem.at[7])
    for c in (in_wide, in_cw, in_damp, in_cls, in_land, in_res):
        c.start()
    in_order.wait()

    row = iota((128, WIDE), 0)
    lane = iota((128, WIDE), 1)
    order_row = jnp.where((row & 32) == 0, order_s[2 * o], order_s[2 * o + 1])
    valid = (lane < DEG) & (lane + l * DEG >= order_row)

    def natural(ref, c):
        return jnp.concatenate(
            [
                ref[m, s, (2 * c + h) * KS : (2 * c + h + 1) * KS, :]
                for h in range(2)
                for m in range(2)
                for s in range(2)
            ],
            axis=0,
        )

    def rows_of(x):
        return wide_to_tall(jnp.where(odd == 1, pltpu.roll(x, 4, 1), x))[0:SLOT]

    in_dir.wait()
    for c in range(CH):
        dn[c, :, 512:WIDE] = jnp.zeros((128, 128), F32)
        dn[c, :, 0:DEG] = natural(dir_v, c)
        g[c, l] = rows_of(jnp.where(valid, dn[c], 0.0))

    pl.semaphore_wait(barrier, NO - 1 + NL - 1)

    def ag(c, k, slot, lo, to):
        return pltpu.make_async_remote_copy(
            src_ref=g.at[c, slot, pl.ds(lo, HALF), :],
            dst_ref=g.at[c, slot, pl.ds(lo, HALF), :],
            send_sem=ag_s.at[c, k],
            recv_sem=ag_r.at[c, k],
            device_id=(o, to),
            device_id_type=MESH,
        )

    def ag_first(c):
        ag(c, 0, l, 0, right).start()
        ag(c, 1, l, HALF, left).start()
        ag(c, 2, l, HALF, right).start()
        ag(c, 3, l, 0, left).start()

    def ag_forward(c):
        ag(c, 0, left, 0, right).wait_recv()
        ag(c, 4, left, 0, right).start()
        ag(c, 1, right, HALF, left).wait_recv()
        ag(c, 5, right, HALF, left).start()

    ag_first(0)

    def convert(b, m):
        leg_in[2 * b + m].wait()

        def body(i, carry):
            at = pl.ds(pl.multiple_of(i * 32, 32), 32)
            hi, lo = split(lf[m, b, at, :])
            lh[m, b, at, :] = hi
            ll[m, b, at, :] = lo
            return carry

        lax.fori_loop(0, SLOT // 32, body, 0)

    for b in range(NL):
        for m in range(2):
            convert(b, m)

    in_wide.wait()
    in_cw.wait()
    in_damp.wait()
    col = iota((128, 256), 1)
    pick = (iota((128, 256), 0) == 2 * (col & 63) + (col >> 7)).astype(F32)
    sixteenth = jnp.broadcast_to(order_v[...].astype(F32) * (1.0 / 16.0), (8, 128))
    orders = mm(sixteenth.astype(BF16), pick.astype(BF16))[0:1, :] * 16.0
    j = iota((384, 256), 0).astype(F32)
    turns = j * orders
    phase = turns - jnp.floor(turns * (1.0 / NLON)) * float(NLON)
    part = (iota((384, 256), 1) >> 6) & 1
    phase = phase - jnp.where(part == 1, float(NLON // 4), 0.0)
    table = jnp.cos(phase * (2.0 * math.pi / NLON))
    hi, lo = split(table)
    hth[...] = hi[0:ROWS_J]
    htl[...] = lo[0:ROWS_J]
    flat = jnp.concatenate([tall_to_wide(table[:, 0:128]), tall_to_wide(table[:, 128:256])], 0)
    hi, lo = split(flat)
    hh[...] = hi[:, 0:ROWS_J]
    hl[...] = lo[:, 0:ROWS_J]

    in_cls.wait()
    in_land.wait()
    wv[:, 4224:4608] = jnp.zeros((8, 384), F32)
    for lo_lane in range(0, NLON, 640):
        n = min(640, NLON - lo_lane)
        cls = cls_v[:, lo_lane : lo_lane + n]
        on_land = land_v[:, lo_lane : lo_lane + n] == 1
        w = jnp.zeros((8, n), F32)
        for k in range(16):
            w = jnp.where(cls == k, jnp.where(on_land, cw_s[1, k], cw_s[0, k]), w)
        wv[:, lo_lane : lo_lane + n] = w
    folded = jnp.zeros((8, 512), F32)
    for i in range(NLON // PERIOD):
        base = PERIOD * i // 128 * 128
        off = PERIOD * i - base
        v = wv[:, base : base + 512]
        if off:
            v = pltpu.roll(v, 512 - off, 1)
        folded = folded + v
    folded = jnp.where(iota((8, 512), 1) < PERIOD, folded, 0.0) * (2.0 / NLON)
    folded = jnp.concatenate([folded[:, 0:384], jnp.zeros((120, 384), F32)], axis=0)
    spread = (iota((128, 128), 0) == (iota((128, 128), 1) >> 4)).astype(F32)
    wx[...] = jnp.dot(
        wide_to_tall(folded), spread, precision=lax.Precision.HIGHEST, preferred_element_type=F32
    )[0:ROWS_J]

    ag_forward(0)
    ag_first(1)

    norms = []
    damped = []

    def prepare():
        dampp[:, 512:WIDE] = jnp.zeros((1, 128), F32)
        dampp[:, 0:DEG] = damp_v[...].reshape(1, DEG)
        x = rows_of(jnp.broadcast_to(dampp[...], (128, WIDE)))
        dampt[...] = pack(x, 0)
        validt[...] = pack(rows_of(valid.astype(F32)), 0)
        in_res.wait()
        for c in range(CH):
            dn[c, :, 0:DEG] = natural(res_v, c)
            x = rows_of(jnp.where(valid, dn[c], 0.0))
            y = g[c, l]
            for h in range(2):
                xh, yh = pack(x, h), pack(y, h)
                rt[2 * c + h] = xh
                gp[2 * c + h] = yh
                norms.append(jnp.sum(xh * xh, axis=0, keepdims=True))
                damped.append(jnp.sum(yh * (yh * dampt[...]), axis=0, keepdims=True))

    def synth(c, slot, first):
        x = jnp.concatenate([g[c, slot], jnp.zeros((WIDE - SLOT, 128), F32)], axis=0)
        wide = tall_to_wide(x)[:, 0:SLOT]
        hi, lo = split(wide)
        for m in range(2):
            a = 32 * m
            hi_m = jnp.concatenate([hi[a : a + 32], hi[a + 64 : a + 96]], axis=0)
            lo_m = jnp.concatenate([lo[a : a + 32], lo[a + 64 : a + 96]], axis=0)
            both = mm(jnp.concatenate([hi_m, lo_m], axis=0), lh[m, slot])
            out = both[0:64] + both[64:128] + mm(hi_m, ll[m, slot])
            for h in range(2):
                at = slice(a + 64 * h, a + 64 * h + 32)
                part = out[32 * h : 32 * h + 32]
                rs_acc[at, :] = part if first else rs_acc[at, :] + part

    def all_to_all(src, dst, i, ssem, rsem):
        def body(k, carry):
            peer = order_peer(k)
            pltpu.make_async_remote_copy(
                src_ref=src.at[i, peer],
                dst_ref=dst.at[i, o],
                send_sem=ssem.at[i],
                recv_sem=rsem.at[i],
                device_id=(peer, l),
                device_id_type=MESH,
            ).start()
            return carry

        lax.fori_loop(0, NO - 1, body, 0, unroll=9)
        dst[i, o] = src[i, o]

    def take_all(ref, i, sem):
        part_ref = ref.at[i, pl.ds(0, NO - 1)]
        pltpu.make_async_copy(part_ref, part_ref, sem.at[i]).wait()

    low_o = iota((NO, 128), 1) < 64
    group = (iota((NO, 128), 1) >> 4) & 3

    def synth_near(c):
        synth(c, l, True)
        ag(c, 2, left, HALF, right).wait_recv()
        synth(c, left, False)
        ag(c, 3, right, 0, left).wait_recv()
        synth(c, right, False)

    def synth_far(c):
        ag(c, 4, opp, 0, right).wait_recv()
        ag(c, 5, opp, HALF, left).wait_recv()
        synth(c, opp, False)
        xs[...] = wide_to_tall(rs_acc[...])
        for rr in range(4):
            x = xs[pl.ds(rr, NO, stride=8), :]
            y = xs[pl.ds(rr + 4, NO, stride=8), :]
            sy[2 * c, :, rr, :] = jnp.where(low_o, x, pltpu.roll(y, 64, 1))
            sy[2 * c + 1, :, rr, :] = jnp.where(low_o, pltpu.roll(x, 64, 1), y)

    def exchange(i):
        all_to_all(sy, r, i, a2_s, a2_r)

    def reduce_start(i, value):
        v1[i, o] = value

        def body(k, carry):
            peer = order_peer(k)
            pltpu.make_async_remote_copy(
                src_ref=v1.at[i, o],
                dst_ref=v1.at[i, o],
                send_sem=v1_s.at[i],
                recv_sem=v1_r.at[i],
                device_id=(peer, l),
                device_id_type=MESH,
            ).start()
            return carry

        lax.fori_loop(0, NO - 1, body, 0, unroll=9)

    def v2_copy(i, k):
        return pltpu.make_async_remote_copy(
            src_ref=v2.at[i, l],
            dst_ref=v2.at[i, l],
            send_sem=v2_s.at[i],
            recv_sem=v2_r.at[i],
            device_id=(o, lax.rem(l + k, NL)),
            device_id_type=MESH,
        )

    def reduce_middle(i):
        got = v1.at[i, pl.ds(0, NO - 1)]
        pltpu.make_async_copy(got, got, v1_r.at[i]).wait()
        v2[i, l] = jnp.sum(v1[i], axis=0)
        for k in range(1, NL):
            v2_copy(i, k).start()

    def reduce_end(i):
        got = v2.at[i, pl.ds(0, NL - 1)]
        pltpu.make_async_copy(got, got, v2_r.at[i]).wait()
        return jnp.sum(v2[i], axis=0)

    curves = [None] * NS

    def grid_stage(i):
        take_all(r, i, a2_r)
        parts = [None] * 4
        for rr in range(4):
            x = r[i, :, rr, :]
            for p in range(4):
                y = pltpu.roll(x, 16 * (rr - p) % 128, 1) if rr != p else x
                parts[p] = y if rr == 0 else jnp.where(group == rr, y, parts[p])
        hi, lo = split(jnp.concatenate(parts, axis=0))
        both = mm(hth[...], jnp.concatenate([hi, lo], axis=1))
        surface = both[:, 0:128] + (both[:, 128:256] + mm(htl[...], hi))
        weighted = wx[...] * surface
        curves[i] = jnp.sum(weighted * surface, axis=0, keepdims=True)
        hi, lo = split(weighted)
        both = mm(hh[...], jnp.concatenate([hi, lo], axis=1))
        spectra = both[:, 0:128] + (both[:, 128:256] + mm(hl[...], hi))
        for rr in range(4):
            y = None
            for p in range(4):
                x = spectra[64 * p : 64 * p + 64]
                if rr != p:
                    x = pltpu.roll(x, 16 * (p - rr) % 128, 1)
                y = x if y is None else jnp.where(group == p, x, y)
            t[i, :, rr, :] = y
        all_to_all(t, q, i, b2_s, b2_r)

    octant = iota((1, 128), 1) >> 4

    def join(rows):
        x = jnp.zeros((1, 128), F32)
        for k, y in enumerate(rows):
            x = jnp.where(octant == k, fold8(y), x)
        return x

    def part_of(x, k):
        return fold8(jnp.where(octant == k, x, 0.0))

    def sums_start():
        reduce_start(0, join(norms + [curves[i] + damped[i] for i in range(NS)]))

    low = iota((PACK, 128), 1) < 64
    low_t = iota((BAND, 128), 1) < 64
    first_m = (iota((SLOT, 128), 1) & 32) == 0

    def analysis_operands(i):
        take_all(q, i, b2_r)
        for rr in range(4):
            x = q[i, :, rr, :]
            xs[pl.ds(rr, NO, stride=8), :] = x
            xs[pl.ds(rr + 4, NO, stride=8), :] = pltpu.roll(x, 64, 1)
        hi, lo = split(xs[...])
        hif = hi.astype(F32)
        lof = pltpu.roll(lo.astype(F32), 64, 1)
        one = jnp.where(low_t, hif, lof).astype(BF16)
        two = jnp.where(low_t, hif, 0.0).astype(BF16)
        return one, two

    def analysis(i, slot, operands):
        one, two = operands
        p0, p1 = mm(lh[0, slot], one), mm(lh[1, slot], one)
        t0, t1 = mm(ll[0, slot], two), mm(ll[1, slot], two)
        x = jnp.where(first_m, p0, p1) + jnp.where(first_m, t0, t1)
        x = x + pltpu.roll(x, 64, 1)
        pp[i, slot] = jnp.where(low, x[0:PACK], x[PACK:SLOT])

    def rs_one(c, k, lo, to):
        return pltpu.make_async_remote_copy(
            src_ref=pp.at[c, opp, pl.ds(lo, QH), :],
            dst_ref=ra.at[c, k],
            send_sem=rs_s.at[c, k],
            recv_sem=rs_r.at[c, k],
            device_id=(o, to),
            device_id_type=MESH,
        )

    def rs_two(c, k, side, slot, lo, to):
        return pltpu.make_async_remote_copy(
            src_ref=pp.at[c, slot, pl.ds(lo, QH), :],
            dst_ref=rb.at[c, side, pl.ds(lo, QH), :],
            send_sem=rs_s.at[c, k],
            recv_sem=rs_r.at[c, k],
            device_id=(o, to),
            device_id_type=MESH,
        )

    def scatter_start(c):
        operands = analysis_operands(c)
        analysis(c, opp, operands)
        rs_one(c, 0, 0, right).start()
        rs_one(c, 1, QH, left).start()
        analysis(c, right, operands)
        rs_two(c, 2, 0, right, QH, right).start()
        analysis(c, left, operands)
        rs_two(c, 3, 1, left, 0, left).start()
        analysis(c, l, operands)

    def scatter_middle(c):
        rs_one(c, 0, 0, right).wait_recv()
        pp[c, right, 0:QH, :] = pp[c, right, 0:QH, :] + ra[c, 0]
        rs_two(c, 4, 0, right, 0, right).start()
        rs_one(c, 1, QH, left).wait_recv()
        pp[c, left, QH:PACK, :] = pp[c, left, QH:PACK, :] + ra[c, 1]
        rs_two(c, 5, 1, left, QH, left).start()

    def scatter_end(i):
        before, curve = sums[i]
        rs_two(i, 2, 0, right, QH, right).wait_recv()
        rs_two(i, 3, 1, left, 0, left).wait_recv()
        rs_two(i, 4, 0, right, 0, right).wait_recv()
        rs_two(i, 5, 1, left, QH, left).wait_recv()
        x = pp[i, l] + (rb[i, 0] + rb[i, 1])
        step = before / curve
        applied = jnp.where(validt[...] > 0.5, x + dampt[...] * gp[i], 0.0)
        new_res = rt[i] - step * applied
        after[i] = jnp.sum(new_res * new_res, axis=0, keepdims=True)
        return step, applied

    def scatter_out(i, step, applied):
        x = jnp.concatenate([applied, jnp.zeros((384 - PACK, 128), F32)], axis=0)
        x = tall_to_wide(x)
        zero = jnp.zeros((64, WIDE - 384), F32)
        x = jnp.concatenate([x[0:64], zero], axis=1) + pltpu.roll(
            jnp.concatenate([x[64:128], zero], axis=1), PACK, 1
        )
        x = jnp.where(odd == 1, pltpu.roll(x, WIDE - 4, 1), x)
        for p in range(4):
            app_v[p // 2, p % 2, i * KS : (i + 1) * KS, :] = x[16 * p : 16 * p + 16, 0:DEG]
        cols_v[0, i * KS : (i + 1) * KS, :] = column(step)[0:KS]

    sums = [None] * NS
    after = [None] * NS

    def sums_end():
        got = reduce_end(0)
        for i in range(NS):
            sums[i] = (part_of(got, i), part_of(got, NS + i))

    def norm_start():
        reduce_start(1, join(after))

    def finish():
        got = reduce_end(1)
        for i in range(NS):
            ratio = column(part_of(got, i) / sums[i][0])
            cols_v[1, i * KS : (i + 1) * KS, :] = ratio[0:KS]

    def drain():
        for c in range(CH):
            ag(c, 0, l, 0, right).wait_send()
            ag(c, 1, l, HALF, left).wait_send()
            ag(c, 2, l, HALF, right).wait_send()
            ag(c, 3, l, 0, left).wait_send()
            ag(c, 4, left, 0, right).wait_send()
            ag(c, 5, right, HALF, left).wait_send()
        for i in range(NS):
            rs_one(i, 0, 0, right).wait_send()
            rs_one(i, 1, QH, left).wait_send()
            rs_two(i, 2, 0, right, QH, right).wait_send()
            rs_two(i, 3, 1, left, 0, left).wait_send()
            rs_two(i, 4, 0, right, 0, right).wait_send()
            rs_two(i, 5, 1, left, QH, left).wait_send()
            take_all(sy, i, a2_s)
            take_all(t, i, b2_s)

    prepare()
    synth_near(0)
    synth_far(0)
    exchange(0)
    exchange(1)
    ag_forward(1)
    synth_near(1)
    grid_stage(0)
    synth_far(1)
    exchange(2)
    grid_stage(1)
    exchange(3)
    scatter_start(0)
    grid_stage(2)
    scatter_middle(0)
    scatter_start(1)
    grid_stage(3)
    sums_start()
    scatter_middle(1)
    scatter_start(2)
    scatter_start(3)
    scatter_middle(2)
    reduce_middle(0)
    sums_end()
    out0 = scatter_end(0)
    out1 = scatter_end(1)
    scatter_middle(3)
    out2 = scatter_end(2)
    out3 = scatter_end(3)
    norm_start()
    scatter_out(0, *out0)
    scatter_out(1, *out1)
    scatter_out(2, *out2)
    scatter_out(3, *out3)
    out_app = pltpu.make_async_copy(app_v, app_h, osem.at[0])
    out_app.start()
    drain()
    reduce_middle(1)
    finish()

    for i in range(2):
        sent = v1.at[i, pl.ds(0, NO - 1)]
        pltpu.make_async_copy(sent, sent, v1_s.at[i]).wait()
        sent = v2.at[i, pl.ds(0, NL - 1)]
        pltpu.make_async_copy(sent, sent, v2_s.at[i]).wait()
    out_app.wait()


def combine(pos_v, res_v, dir_v, app_v, order_s, cols_v, npos_h, nres_h, ndir_h, y, osem):
    o = lax.axis_index("order")
    l = lax.axis_index("lat")
    degree = iota((64, DEG), 1) + l * DEG
    step = jnp.concatenate([cols_v[0]] * 5, axis=1)[:, 0:DEG]
    ratio = jnp.concatenate([cols_v[1]] * 5, axis=1)[:, 0:DEG]
    outs = []
    for m in range(2):
        valid = degree >= order_s[2 * o + m]
        for s in range(2):
            pos, res, way = (jnp.where(valid, x[m, s], 0.0) for x in (pos_v, res_v, dir_v))
            new_res = res - step * app_v[m, s]
            y[0, m, s] = pos + step * way
            y[1, m, s] = new_res
            y[2, m, s] = new_res + ratio * way
            for k, ref in enumerate((npos_h, nres_h, ndir_h)):
                c = pltpu.make_async_copy(y.at[k, m, s], ref.at[m, s], osem.at[k, m, s])
                c.start()
                outs.append(c)
    for c in outs:
        c.wait()


def shards(
    position, residual, direction, legendre, order_of, class_idx, land, class_weight, damping
):
    any_spec = pl.BlockSpec(memory_space=pl.ANY)
    hbm = pl.BlockSpec(memory_space=pltpu.HBM)
    smem = pl.BlockSpec(memory_space=pltpu.SMEM)
    vmem = pl.BlockSpec(memory_space=pltpu.VMEM)
    dma = pltpu.SemaphoreType.DMA
    block = (2, 2, 64, DEG)
    applied, columns = pl.pallas_call(
        kernel,
        out_shape=[jax.ShapeDtypeStruct(block, F32), jax.ShapeDtypeStruct((2, 64, 128), F32)],
        in_specs=[hbm] * 9,
        out_specs=[any_spec, vmem],
        scratch_shapes=[
            pltpu.SMEM((128,), jnp.int32),
            pltpu.VMEM((1, 128), jnp.int32),
            pltpu.SMEM((2, 16), F32),
            pltpu.VMEM((DEG,), F32),
            pltpu.VMEM((2, NL, SLOT, BAND), F32),
            pltpu.VMEM((2, NL, SLOT, BAND), BF16),
            pltpu.VMEM((2, NL, SLOT, BAND), BF16),
            pltpu.VMEM(block, F32),
            pltpu.VMEM(block, F32),
            pltpu.VMEM(block, F32),
            pltpu.VMEM((8, NLON), jnp.int32),
            pltpu.VMEM((8, NLON), jnp.int32),
            pltpu.VMEM((8, 4608), F32),
            pltpu.VMEM((CH, 128, WIDE), F32),
            pltpu.VMEM((1, WIDE), F32),
            pltpu.VMEM((CH, NL, SLOT, 128), F32),
            pltpu.VMEM((NS, PACK, 128), F32),
            pltpu.VMEM((BAND, 128), F32),
            pltpu.VMEM((NS, NO, 4, 128), F32),
            pltpu.VMEM((NS, NO, 4, 128), F32),
            pltpu.VMEM((NS, NO, 4, 128), F32),
            pltpu.VMEM((NS, NO, 4, 128), F32),
            pltpu.VMEM((NS, NL, PACK, 128), F32),
            pltpu.VMEM((NS, 2, QH, 128), F32),
            pltpu.VMEM((NS, 2, PACK, 128), F32),
            pltpu.VMEM((2, NO, 1, 128), F32),
            pltpu.VMEM((2, NL, 1, 128), F32),
            pltpu.VMEM((NS, PACK, 128), F32),
            pltpu.VMEM((PACK, 128), F32),
            pltpu.VMEM((PACK, 128), F32),
            pltpu.VMEM((ROWS_J, 256), BF16),
            pltpu.VMEM((ROWS_J, 256), BF16),
            pltpu.VMEM((256, ROWS_J), BF16),
            pltpu.VMEM((256, ROWS_J), BF16),
            pltpu.VMEM((ROWS_J, 128), F32),
            pltpu.VMEM((128, BAND), F32),
            dma((8,)),
            dma((8,)),
            dma((3,)),
            dma((CH, 6)),
            dma((CH, 6)),
            dma((NS,)),
            dma((NS,)),
            dma((NS,)),
            dma((NS,)),
            dma((NS, 6)),
            dma((NS, 6)),
            dma((2,)),
            dma((2,)),
            dma((2,)),
            dma((2,)),
        ],
        compiler_params=pltpu.CompilerParams(
            collective_id=0, has_side_effects=True, vmem_limit_bytes=36 * 1024 * 1024
        ),
        name="cg_iteration",
    )(
        *(
            pltpu.with_memory_space_constraint(a, pltpu.HBM)
            for a in (
                residual, direction, legendre, class_idx, land,
                order_of, order_of.reshape(1, -1), class_weight.T, damping,
            )
        )
    )
    return pl.pallas_call(
        combine,
        out_shape=[jax.ShapeDtypeStruct(block, F32)] * 3,
        in_specs=[vmem] * 4 + [smem, vmem],
        out_specs=[any_spec] * 3,
        scratch_shapes=[
            pltpu.VMEM((3,) + block, F32),
            dma((3, 2, 2)),
        ],
        compiler_params=pltpu.CompilerParams(vmem_limit_bytes=16 * 1024 * 1024),
        name="combine",
    )(position, residual, direction, applied, order_of, columns)


def solution(mesh):
    return jax.shard_map(
        shards,
        mesh=mesh,
        in_specs=(
            P("order", None, None, "lat"),
            P("order", None, None, "lat"),
            P("order", None, None, "lat"),
            P("order", None, "lat"),
            P(),
            P(("lat", "order"), None),
            P(("lat", "order"), None),
            P(),
            P("lat"),
        ),
        out_specs=(
            P("order", None, None, "lat"),
            P("order", None, None, "lat"),
            P("order", None, None, "lat"),
        ),
        check_vma=False,
    )
```

```python
import functools
import math

import jax
import jax.numpy as jnp
from jax import lax
from jax.experimental import pallas as pl
from jax.experimental.pallas import tpu as pltpu
from jax.sharding import PartitionSpec as P

F32 = jnp.float32
BF16 = jnp.bfloat16
MESH = pl.DeviceIdType.MESH

NO = 64
NL = 4
DEG = 540
SLOT = 544
HALF = SLOT // 2
WIDE = 640
STARTS = (0, 536, 1080, 1616)
BAND = 512
CH = 2
NS = 4
KS = 16
PACK = SLOT // 2
QH = PACK // 2
PERIOD = 270
NLON = 4320
ROWS_J = 272


def tall_to_wide(x):
    n = x.shape[0] // 128
    return jnp.concatenate([x[128 * i : 128 * (i + 1)].T for i in range(n)], axis=1)


def wide_to_tall(x):
    n = x.shape[1] // 128
    return jnp.concatenate([x[:, 128 * i : 128 * (i + 1)].T for i in range(n)], axis=0)


def split(x):
    hi = x.astype(BF16)
    lo = (x - hi.astype(F32)).astype(BF16)
    return hi, lo


def mm(a, b):
    return jnp.dot(a, b, preferred_element_type=F32)


def iota(shape, axis):
    return lax.broadcasted_iota(jnp.int32, shape, axis)


def fold8(x):
    y = x + pltpu.roll(x, 64, 1)
    y = y + pltpu.roll(y, 32, 1)
    return y + pltpu.roll(y, 16, 1)


def pack(x, h):
    low = iota((PACK, 128), 1) < 64
    top, bottom = x[0:PACK], x[PACK:SLOT]
    if h == 0:
        return jnp.where(low, top, pltpu.roll(bottom, 64, 1))
    return jnp.where(low, pltpu.roll(top, 64, 1), bottom)


def column(row):
    return jnp.broadcast_to(row, (128, 128)).T


def kernel(
    res_h, dir_h, leg_h, cls_h, land_h, order_h, order_w, cw_h, damp_h,
    app_h, cols_v, order_s, order_v, cw_s, damp_v,
    lf, lh, ll, dir_v, res_v, app_v, cls_v, land_v, wv,
    dn, dampp, g, gp, xs, sy, r, t, q, pp, ra, rb, v1, v2,
    rt, dampt, validt, hth, htl, hh, hl, wx, rs_acc,
    lsem, isem, osem, ag_s, ag_r, a2_s, a2_r, b2_s, b2_r, rs_s, rs_r, v1_s, v1_r, v2_s, v2_r,
):
    o = lax.axis_index("order")
    l = lax.axis_index("lat")
    right = lax.rem(l + 1, NL)
    left = lax.rem(l + NL - 1, NL)
    opp = lax.rem(l + 2, NL)
    odd = lax.rem(l, 2)

    in_dir = pltpu.make_async_copy(dir_h, dir_v, isem.at[0])
    in_dir.start()
    in_order = pltpu.make_async_copy(order_h, order_s, isem.at[2])
    in_order.start()
    barrier = pltpu.get_barrier_semaphore()

    def order_peer(i):
        k = i >> 3
        dz = 4 + ((k + 1) >> 1) * (1 - 2 * (k & 1))
        j = (i & 7) + ((k + 1) >> 3)
        return ((o + dz * 8) & 56) + ((o + j) & 7)

    def greet(i, carry):
        pl.semaphore_signal(
            barrier, inc=1, device_id=(order_peer(i), l), device_id_type=MESH
        )
        return carry

    for i in range(1, NL):
        pl.semaphore_signal(
            barrier, inc=1, device_id=(o, lax.rem(l + i, NL)), device_id_type=MESH
        )
    lax.fori_loop(0, NO - 1, greet, 0, unroll=9)

    leg_in = []
    for b in range(NL):
        for m in range(2):
            c = pltpu.make_async_copy(
                leg_h.at[m, pl.ds(STARTS[b], SLOT), :], lf.at[m, b], lsem.at[2 * b + m]
            )
            c.start()
            leg_in.append(c)
    in_res = pltpu.make_async_copy(res_h, res_v, isem.at[1])
    in_cls = pltpu.make_async_copy(cls_h, cls_v, isem.at[3])
    in_land = pltpu.make_async_copy(land_h, land_v, isem.at[4])
    in_wide = pltpu.make_async_copy(order_w, order_v, isem.at[5])
    in_cw = pltpu.make_async_copy(cw_h, cw_s, isem.at[6])
    in_damp = pltpu.make_async_copy(damp_h, damp_v, isem.at[7])
    for c in (in_wide, in_cw, in_damp, in_cls, in_land, in_res):
        c.start()
    in_order.wait()

    row = iota((128, WIDE), 0)
    lane = iota((128, WIDE), 1)
    order_row = jnp.where((row & 32) == 0, order_s[2 * o], order_s[2 * o + 1])
    valid = (lane < DEG) & (lane + l * DEG >= order_row)

    def natural(ref, c):
        return jnp.concatenate(
            [
                ref[m, s, (2 * c + h) * KS : (2 * c + h + 1) * KS, :]
                for h in range(2)
                for m in range(2)
                for s in range(2)
            ],
            axis=0,
        )

    def rows_of(x):
        return wide_to_tall(jnp.where(odd == 1, pltpu.roll(x, 4, 1), x))[0:SLOT]

    in_dir.wait()
    for c in range(CH):
        dn[c, :, 512:WIDE] = jnp.zeros((128, 128), F32)
        dn[c, :, 0:DEG] = natural(dir_v, c)
        g[c, l] = rows_of(jnp.where(valid, dn[c], 0.0))

    pl.semaphore_wait(barrier, NO - 1 + NL - 1)

    def ag(c, k, slot, lo, to):
        return pltpu.make_async_remote_copy(
            src_ref=g.at[c, slot, pl.ds(lo, HALF), :],
            dst_ref=g.at[c, slot, pl.ds(lo, HALF), :],
            send_sem=ag_s.at[c, k],
            recv_sem=ag_r.at[c, k],
            device_id=(o, to),
            device_id_type=MESH,
        )

    def ag_first(c):
        ag(c, 0, l, 0, right).start()
        ag(c, 1, l, HALF, left).start()
        ag(c, 2, l, HALF, right).start()
        ag(c, 3, l, 0, left).start()

    def ag_forward(c):
        ag(c, 0, left, 0, right).wait_recv()
        ag(c, 4, left, 0, right).start()
        ag(c, 1, right, HALF, left).wait_recv()
        ag(c, 5, right, HALF, left).start()

    ag_first(0)

    def convert(b, m):
        leg_in[2 * b + m].wait()

        def body(i, carry):
            at = pl.ds(pl.multiple_of(i * 32, 32), 32)
            hi, lo = split(lf[m, b, at, :])
            lh[m, b, at, :] = hi
            ll[m, b, at, :] = lo
            return carry

        lax.fori_loop(0, SLOT // 32, body, 0)

    for b in range(NL):
        for m in range(2):
            convert(b, m)

    in_wide.wait()
    in_cw.wait()
    in_damp.wait()
    col = iota((128, 256), 1)
    pick = (iota((128, 256), 0) == 2 * (col & 63) + (col >> 7)).astype(F32)
    sixteenth = jnp.broadcast_to(order_v[...].astype(F32) * (1.0 / 16.0), (8, 128))
    orders = mm(sixteenth.astype(BF16), pick.astype(BF16))[0:1, :] * 16.0
    j = iota((384, 256), 0).astype(F32)
    turns = j * orders
    phase = turns - jnp.floor(turns * (1.0 / NLON)) * float(NLON)
    part = (iota((384, 256), 1) >> 6) & 1
    phase = phase - jnp.where(part == 1, float(NLON // 4), 0.0)
    table = jnp.cos(phase * (2.0 * math.pi / NLON))
    hi, lo = split(table)
    hth[...] = hi[0:ROWS_J]
    htl[...] = lo[0:ROWS_J]
    flat = jnp.concatenate([tall_to_wide(table[:, 0:128]), tall_to_wide(table[:, 128:256])], 0)
    hi, lo = split(flat)
    hh[...] = hi[:, 0:ROWS_J]
    hl[...] = lo[:, 0:ROWS_J]

    in_cls.wait()
    in_land.wait()
    wv[:, 4224:4608] = jnp.zeros((8, 384), F32)
    for lo_lane in range(0, NLON, 640):
        n = min(640, NLON - lo_lane)
        cls = cls_v[:, lo_lane : lo_lane + n]
        on_land = land_v[:, lo_lane : lo_lane + n] == 1
        w = jnp.zeros((8, n), F32)
        for k in range(16):
            w = jnp.where(cls == k, jnp.where(on_land, cw_s[1, k], cw_s[0, k]), w)
        wv[:, lo_lane : lo_lane + n] = w
    folded = jnp.zeros((8, 512), F32)
    for i in range(NLON // PERIOD):
        base = PERIOD * i // 128 * 128
        off = PERIOD * i - base
        v = wv[:, base : base + 512]
        if off:
            v = pltpu.roll(v, 512 - off, 1)
        folded = folded + v
    folded = jnp.where(iota((8, 512), 1) < PERIOD, folded, 0.0) * (2.0 / NLON)
    folded = jnp.concatenate([folded[:, 0:384], jnp.zeros((120, 384), F32)], axis=0)
    spread = (iota((128, 128), 0) == (iota((128, 128), 1) >> 4)).astype(F32)
    wx[...] = jnp.dot(
        wide_to_tall(folded), spread, precision=lax.Precision.HIGHEST, preferred_element_type=F32
    )[0:ROWS_J]

    ag_forward(0)
    ag_first(1)

    norms = []
    damped = []

    def prepare():
        dampp[:, 512:WIDE] = jnp.zeros((1, 128), F32)
        dampp[:, 0:DEG] = damp_v[...].reshape(1, DEG)
        x = rows_of(jnp.broadcast_to(dampp[...], (128, WIDE)))
        dampt[...] = pack(x, 0)
        validt[...] = pack(rows_of(valid.astype(F32)), 0)
        in_res.wait()
        for c in range(CH):
            dn[c, :, 0:DEG] = natural(res_v, c)
            x = rows_of(jnp.where(valid, dn[c], 0.0))
            y = g[c, l]
            for h in range(2):
                xh, yh = pack(x, h), pack(y, h)
                rt[2 * c + h] = xh
                gp[2 * c + h] = yh
                norms.append(jnp.sum(xh * xh, axis=0, keepdims=True))
                damped.append(jnp.sum(yh * (yh * dampt[...]), axis=0, keepdims=True))

    def synth(c, slot, first):
        x = jnp.concatenate([g[c, slot], jnp.zeros((WIDE - SLOT, 128), F32)], axis=0)
        wide = tall_to_wide(x)[:, 0:SLOT]
        hi, lo = split(wide)
        for m in range(2):
            a = 32 * m
            hi_m = jnp.concatenate([hi[a : a + 32], hi[a + 64 : a + 96]], axis=0)
            lo_m = jnp.concatenate([lo[a : a + 32], lo[a + 64 : a + 96]], axis=0)
            both = mm(jnp.concatenate([hi_m, lo_m], axis=0), lh[m, slot])
            out = both[0:64] + both[64:128] + mm(hi_m, ll[m, slot])
            for h in range(2):
                at = slice(a + 64 * h, a + 64 * h + 32)
                part = out[32 * h : 32 * h + 32]
                rs_acc[at, :] = part if first else rs_acc[at, :] + part

    def all_to_all(src, dst, i, ssem, rsem):
        def body(k, carry):
            peer = order_peer(k)
            pltpu.make_async_remote_copy(
                src_ref=src.at[i, peer],
                dst_ref=dst.at[i, o],
                send_sem=ssem.at[i],
                recv_sem=rsem.at[i],
                device_id=(peer, l),
                device_id_type=MESH,
            ).start()
            return carry

        lax.fori_loop(0, NO - 1, body, 0, unroll=9)
        dst[i, o] = src[i, o]

    def take_all(ref, i, sem):
        part_ref = ref.at[i, pl.ds(0, NO - 1)]
        pltpu.make_async_copy(part_ref, part_ref, sem.at[i]).wait()

    low_o = iota((NO, 128), 1) < 64
    group = (iota((NO, 128), 1) >> 4) & 3

    def synth_near(c):
        synth(c, l, True)
        ag(c, 2, left, HALF, right).wait_recv()
        synth(c, left, False)
        ag(c, 3, right, 0, left).wait_recv()
        synth(c, right, False)

    def synth_far(c):
        ag(c, 4, opp, 0, right).wait_recv()
        ag(c, 5, opp, HALF, left).wait_recv()
        synth(c, opp, False)
        xs[...] = wide_to_tall(rs_acc[...])
        for rr in range(4):
            x = xs[pl.ds(rr, NO, stride=8), :]
            y = xs[pl.ds(rr + 4, NO, stride=8), :]
            sy[2 * c, :, rr, :] = jnp.where(low_o, x, pltpu.roll(y, 64, 1))
            sy[2 * c + 1, :, rr, :] = jnp.where(low_o, pltpu.roll(x, 64, 1), y)
        for h in range(2):
            all_to_all(sy, r, 2 * c + h, a2_s, a2_r)

    def reduce_start(i, value):
        v1[i, o] = value

        def body(k, carry):
            peer = order_peer(k)
            pltpu.make_async_remote_copy(
                src_ref=v1.at[i, o],
                dst_ref=v1.at[i, o],
                send_sem=v1_s.at[i],
                recv_sem=v1_r.at[i],
                device_id=(peer, l),
                device_id_type=MESH,
            ).start()
            return carry

        lax.fori_loop(0, NO - 1, body, 0, unroll=9)

    def v2_copy(i, k):
        return pltpu.make_async_remote_copy(
            src_ref=v2.at[i, l],
            dst_ref=v2.at[i, l],
            send_sem=v2_s.at[i],
            recv_sem=v2_r.at[i],
            device_id=(o, lax.rem(l + k, NL)),
            device_id_type=MESH,
        )

    def reduce_middle(i):
        got = v1.at[i, pl.ds(0, NO - 1)]
        pltpu.make_async_copy(got, got, v1_r.at[i]).wait()
        v2[i, l] = jnp.sum(v1[i], axis=0)
        for k in range(1, NL):
            v2_copy(i, k).start()

    def reduce_end(i):
        got = v2.at[i, pl.ds(0, NL - 1)]
        pltpu.make_async_copy(got, got, v2_r.at[i]).wait()
        return jnp.sum(v2[i], axis=0)

    curves = [None] * NS

    def grid_stage(i):
        take_all(r, i, a2_r)
        parts = [None] * 4
        for rr in range(4):
            x = r[i, :, rr, :]
            for p in range(4):
                y = pltpu.roll(x, 16 * (rr - p) % 128, 1) if rr != p else x
                parts[p] = y if rr == 0 else jnp.where(group == rr, y, parts[p])
        hi, lo = split(jnp.concatenate(parts, axis=0))
        both = mm(hth[...], jnp.concatenate([hi, lo], axis=1))
        surface = both[:, 0:128] + (both[:, 128:256] + mm(htl[...], hi))
        weighted = wx[...] * surface
        curves[i] = jnp.sum(weighted * surface, axis=0, keepdims=True)
        hi, lo = split(weighted)
        both = mm(hh[...], jnp.concatenate([hi, lo], axis=1))
        spectra = both[:, 0:128] + (both[:, 128:256] + mm(hl[...], hi))
        for rr in range(4):
            y = None
            for p in range(4):
                x = spectra[64 * p : 64 * p + 64]
                if rr != p:
                    x = pltpu.roll(x, 16 * (p - rr) % 128, 1)
                y = x if y is None else jnp.where(group == p, x, y)
            t[i, :, rr, :] = y
        all_to_all(t, q, i, b2_s, b2_r)

    octant = iota((1, 128), 1) >> 4

    def join(rows):
        x = jnp.zeros((1, 128), F32)
        for k, y in enumerate(rows):
            x = jnp.where(octant == k, fold8(y), x)
        return x

    def part_of(x, k):
        return fold8(jnp.where(octant == k, x, 0.0))

    def sums_start():
        reduce_start(0, join(norms + [curves[i] + damped[i] for i in range(NS)]))

    low = iota((PACK, 128), 1) < 64
    low_t = iota((BAND, 128), 1) < 64
    first_m = (iota((SLOT, 128), 1) & 32) == 0

    def analysis_operands(i):
        take_all(q, i, b2_r)
        for rr in range(4):
            x = q[i, :, rr, :]
            xs[pl.ds(rr, NO, stride=8), :] = x
            xs[pl.ds(rr + 4, NO, stride=8), :] = pltpu.roll(x, 64, 1)
        hi, lo = split(xs[...])
        hif = hi.astype(F32)
        lof = pltpu.roll(lo.astype(F32), 64, 1)
        one = jnp.where(low_t, hif, lof).astype(BF16)
        two = jnp.where(low_t, hif, 0.0).astype(BF16)
        return one, two

    def analysis(i, slot, operands):
        one, two = operands
        p0, p1 = mm(lh[0, slot], one), mm(lh[1, slot], one)
        t0, t1 = mm(ll[0, slot], two), mm(ll[1, slot], two)
        x = jnp.where(first_m, p0, p1) + jnp.where(first_m, t0, t1)
        x = x + pltpu.roll(x, 64, 1)
        pp[i, slot] = jnp.where(low, x[0:PACK], x[PACK:SLOT])

    def rs_one(c, k, lo, to):
        return pltpu.make_async_remote_copy(
            src_ref=pp.at[c, opp, pl.ds(lo, QH), :],
            dst_ref=ra.at[c, k],
            send_sem=rs_s.at[c, k],
            recv_sem=rs_r.at[c, k],
            device_id=(o, to),
            device_id_type=MESH,
        )

    def rs_two(c, k, side, slot, lo, to):
        return pltpu.make_async_remote_copy(
            src_ref=pp.at[c, slot, pl.ds(lo, QH), :],
            dst_ref=rb.at[c, side, pl.ds(lo, QH), :],
            send_sem=rs_s.at[c, k],
            recv_sem=rs_r.at[c, k],
            device_id=(o, to),
            device_id_type=MESH,
        )

    def scatter_start(c):
        operands = analysis_operands(c)
        analysis(c, opp, operands)
        rs_one(c, 0, 0, right).start()
        rs_one(c, 1, QH, left).start()
        analysis(c, right, operands)
        rs_two(c, 2, 0, right, QH, right).start()
        analysis(c, left, operands)
        rs_two(c, 3, 1, left, 0, left).start()
        analysis(c, l, operands)

    def scatter_middle(c):
        rs_one(c, 0, 0, right).wait_recv()
        pp[c, right, 0:QH, :] = pp[c, right, 0:QH, :] + ra[c, 0]
        rs_two(c, 4, 0, right, 0, right).start()
        rs_one(c, 1, QH, left).wait_recv()
        pp[c, left, QH:PACK, :] = pp[c, left, QH:PACK, :] + ra[c, 1]
        rs_two(c, 5, 1, left, QH, left).start()

    def scatter_end(i):
        before, curve = sums[i]
        rs_two(i, 2, 0, right, QH, right).wait_recv()
        rs_two(i, 3, 1, left, 0, left).wait_recv()
        rs_two(i, 4, 0, right, 0, right).wait_recv()
        rs_two(i, 5, 1, left, QH, left).wait_recv()
        x = pp[i, l] + (rb[i, 0] + rb[i, 1])
        step = before / curve
        applied = jnp.where(validt[...] > 0.5, x + dampt[...] * gp[i], 0.0)
        new_res = rt[i] - step * applied
        after[i] = jnp.sum(new_res * new_res, axis=0, keepdims=True)
        return step, applied

    def scatter_out(i, step, applied):
        x = jnp.concatenate([applied, jnp.zeros((384 - PACK, 128), F32)], axis=0)
        x = tall_to_wide(x)
        zero = jnp.zeros((64, WIDE - 384), F32)
        x = jnp.concatenate([x[0:64], zero], axis=1) + pltpu.roll(
            jnp.concatenate([x[64:128], zero], axis=1), PACK, 1
        )
        x = jnp.where(odd == 1, pltpu.roll(x, WIDE - 4, 1), x)
        for p in range(4):
            app_v[p // 2, p % 2, i * KS : (i + 1) * KS, :] = x[16 * p : 16 * p + 16, 0:DEG]
        cols_v[0, i * KS : (i + 1) * KS, :] = column(step)[0:KS]

    sums = [None] * NS
    after = [None] * NS

    def sums_end():
        got = reduce_end(0)
        for i in range(NS):
            sums[i] = (part_of(got, i), part_of(got, NS + i))

    def norm_start():
        reduce_start(1, join(after))

    def finish():
        got = reduce_end(1)
        for i in range(NS):
            ratio = column(part_of(got, i) / sums[i][0])
            cols_v[1, i * KS : (i + 1) * KS, :] = ratio[0:KS]

    prepare()
    synth_near(0)
    synth_far(0)
    ag_forward(1)
    synth_near(1)
    grid_stage(0)
    synth_far(1)
    grid_stage(1)
    scatter_start(0)
    grid_stage(2)
    scatter_middle(0)
    grid_stage(3)
    sums_start()
    scatter_start(1)
    scatter_start(2)
    scatter_middle(1)
    reduce_middle(0)
    scatter_start(3)
    scatter_middle(2)
    sums_end()
    out0 = scatter_end(0)
    out1 = scatter_end(1)
    scatter_middle(3)
    out2 = scatter_end(2)
    out3 = scatter_end(3)
    norm_start()
    scatter_out(0, *out0)
    scatter_out(1, *out1)
    scatter_out(2, *out2)
    scatter_out(3, *out3)
    out_app = pltpu.make_async_copy(app_v, app_h, osem.at[0])
    out_app.start()
    reduce_middle(1)
    finish()

    for c in range(CH):
        ag(c, 0, l, 0, right).wait_send()
        ag(c, 1, l, HALF, left).wait_send()
        ag(c, 2, l, HALF, right).wait_send()
        ag(c, 3, l, 0, left).wait_send()
        ag(c, 4, left, 0, right).wait_send()
        ag(c, 5, right, HALF, left).wait_send()
    for i in range(NS):
        rs_one(i, 0, 0, right).wait_send()
        rs_one(i, 1, QH, left).wait_send()
        rs_two(i, 2, 0, right, QH, right).wait_send()
        rs_two(i, 3, 1, left, 0, left).wait_send()
        rs_two(i, 4, 0, right, 0, right).wait_send()
        rs_two(i, 5, 1, left, QH, left).wait_send()
        take_all(sy, i, a2_s)
        take_all(t, i, b2_s)
    for i in range(2):
        sent = v1.at[i, pl.ds(0, NO - 1)]
        pltpu.make_async_copy(sent, sent, v1_s.at[i]).wait()
        sent = v2.at[i, pl.ds(0, NL - 1)]
        pltpu.make_async_copy(sent, sent, v2_s.at[i]).wait()
    out_app.wait()


def combine(pos_v, res_v, dir_v, app_v, order_s, cols_v, npos_h, nres_h, ndir_h, y, osem):
    o = lax.axis_index("order")
    l = lax.axis_index("lat")
    degree = iota((64, DEG), 1) + l * DEG
    step = jnp.concatenate([cols_v[0]] * 5, axis=1)[:, 0:DEG]
    ratio = jnp.concatenate([cols_v[1]] * 5, axis=1)[:, 0:DEG]
    outs = []
    for m in range(2):
        valid = degree >= order_s[2 * o + m]
        for s in range(2):
            pos, res, way = (jnp.where(valid, x[m, s], 0.0) for x in (pos_v, res_v, dir_v))
            new_res = res - step * app_v[m, s]
            y[0, m, s] = pos + step * way
            y[1, m, s] = new_res
            y[2, m, s] = new_res + ratio * way
            for k, ref in enumerate((npos_h, nres_h, ndir_h)):
                c = pltpu.make_async_copy(y.at[k, m, s], ref.at[m, s], osem.at[k, m, s])
                c.start()
                outs.append(c)
    for c in outs:
        c.wait()


def shards(
    position, residual, direction, legendre, order_of, class_idx, land, class_weight, damping
):
    any_spec = pl.BlockSpec(memory_space=pl.ANY)
    hbm = pl.BlockSpec(memory_space=pltpu.HBM)
    smem = pl.BlockSpec(memory_space=pltpu.SMEM)
    vmem = pl.BlockSpec(memory_space=pltpu.VMEM)
    dma = pltpu.SemaphoreType.DMA
    block = (2, 2, 64, DEG)
    applied, columns = pl.pallas_call(
        kernel,
        out_shape=[jax.ShapeDtypeStruct(block, F32), jax.ShapeDtypeStruct((2, 64, 128), F32)],
        in_specs=[hbm] * 9,
        out_specs=[any_spec, vmem],
        scratch_shapes=[
            pltpu.SMEM((128,), jnp.int32),
            pltpu.VMEM((1, 128), jnp.int32),
            pltpu.SMEM((2, 16), F32),
            pltpu.VMEM((DEG,), F32),
            pltpu.VMEM((2, NL, SLOT, BAND), F32),
            pltpu.VMEM((2, NL, SLOT, BAND), BF16),
            pltpu.VMEM((2, NL, SLOT, BAND), BF16),
            pltpu.VMEM(block, F32),
            pltpu.VMEM(block, F32),
            pltpu.VMEM(block, F32),
            pltpu.VMEM((8, NLON), jnp.int32),
            pltpu.VMEM((8, NLON), jnp.int32),
            pltpu.VMEM((8, 4608), F32),
            pltpu.VMEM((CH, 128, WIDE), F32),
            pltpu.VMEM((1, WIDE), F32),
            pltpu.VMEM((CH, NL, SLOT, 128), F32),
            pltpu.VMEM((NS, PACK, 128), F32),
            pltpu.VMEM((BAND, 128), F32),
            pltpu.VMEM((NS, NO, 4, 128), F32),
            pltpu.VMEM((NS, NO, 4, 128), F32),
            pltpu.VMEM((NS, NO, 4, 128), F32),
            pltpu.VMEM((NS, NO, 4, 128), F32),
            pltpu.VMEM((NS, NL, PACK, 128), F32),
            pltpu.VMEM((NS, 2, QH, 128), F32),
            pltpu.VMEM((NS, 2, PACK, 128), F32),
            pltpu.VMEM((2, NO, 1, 128), F32),
            pltpu.VMEM((2, NL, 1, 128), F32),
            pltpu.VMEM((NS, PACK, 128), F32),
            pltpu.VMEM((PACK, 128), F32),
            pltpu.VMEM((PACK, 128), F32),
            pltpu.VMEM((ROWS_J, 256), BF16),
            pltpu.VMEM((ROWS_J, 256), BF16),
            pltpu.VMEM((256, ROWS_J), BF16),
            pltpu.VMEM((256, ROWS_J), BF16),
            pltpu.VMEM((ROWS_J, 128), F32),
            pltpu.VMEM((128, BAND), F32),
            dma((8,)),
            dma((8,)),
            dma((3,)),
            dma((CH, 6)),
            dma((CH, 6)),
            dma((NS,)),
            dma((NS,)),
            dma((NS,)),
            dma((NS,)),
            dma((NS, 6)),
            dma((NS, 6)),
            dma((2,)),
            dma((2,)),
            dma((2,)),
            dma((2,)),
        ],
        compiler_params=pltpu.CompilerParams(
            collective_id=0, has_side_effects=True, vmem_limit_bytes=36 * 1024 * 1024
        ),
        name="cg_iteration",
    )(
        *(
            pltpu.with_memory_space_constraint(a, pltpu.HBM)
            for a in (
                residual, direction, legendre, class_idx, land,
                order_of, order_of.reshape(1, -1), class_weight.T, damping,
            )
        )
    )
    return pl.pallas_call(
        combine,
        out_shape=[jax.ShapeDtypeStruct(block, F32)] * 3,
        in_specs=[vmem] * 4 + [smem, vmem],
        out_specs=[any_spec] * 3,
        scratch_shapes=[
            pltpu.VMEM((3,) + block, F32),
            dma((3, 2, 2)),
        ],
        compiler_params=pltpu.CompilerParams(vmem_limit_bytes=16 * 1024 * 1024),
        name="combine",
    )(position, residual, direction, applied, order_of, columns)


def solution(mesh):
    return jax.shard_map(
        shards,
        mesh=mesh,
        in_specs=(
            P("order", None, None, "lat"),
            P("order", None, None, "lat"),
            P("order", None, None, "lat"),
            P("order", None, "lat"),
            P(),
            P(("lat", "order"), None),
            P(("lat", "order"), None),
            P(),
            P("lat"),
        ),
        out_specs=(
            P("order", None, None, "lat"),
            P("order", None, None, "lat"),
            P("order", None, None, "lat"),
        ),
        check_vma=False,
    )
```
